256 devices in a mesh: gx: 4 (over x_lo, core), gy: 8 (over x_hi, y), gz: 8 (over z).
Axes of the slice: x: 4 (x_hi: 2, x_lo: 2; x = x_hi * 2 + x_lo), y: 4, z: 8, core: 2. Of those that a mesh axis runs over, the one named last changes fastest.
Arguments:
- hamiltonian: float32 [4, 8, 8, 7, 384, 384], P('gx', 'gy', 'gz'), may hold values from -20 to 20, as said below
- keep_mask: int32 [4, 8, 8, 7], P('gx', 'gy', 'gz'), may hold values from 0 to 1, as said below
Outputs:
- sign_blocks: float32 [4, 8, 8, 7, 384, 384], P('gx', 'gy', 'gz')
The draws below stay inside these ranges and needn't reach their ends.
Inputs may be any that keep to these rules, and one draw needn't show every extreme that they name: `hamiltonian`: entries are real numbers; the blocks are dense. `keep_mask`: slot 0 is 1 for every domain.
All inputs are finite; a program needn't handle non-finite values.
Results may differ from the reference program's by a relative error of at most 0.00025.
Values sent between devices are 32-bit elements; how exact they have to be, the bound alone decides.
A program may use at most 128 MiB of HBM per device.

```python
import math
import jax
import jax.numpy as jnp
from jax import lax

B = 384
ITERS = 1
NX = 4
NY = 8
NZ = 8


def draw_hamiltonian(key, part):
    keys = jax.random.split(key, 5)
    shape = (NX, NY, NZ, 7, B, B)
    noise = jax.random.normal(keys[0], shape, jnp.float32)
    signs = jax.random.randint(keys[1], (NX, NY, NZ, B), 0, 2).astype(jnp.float32) * 2.0 - 1.0
    magnitude = jax.random.uniform(keys[2], (NX, NY, NZ, B), jnp.float32, 0.2, 0.6)
    onsite = signs * magnitude
    identity = jnp.eye(B, dtype=jnp.float32)
    first_slot = (jnp.arange(7) == 0).astype(jnp.float32)
    matrix = 0.02 * noise + first_slot[:, None, None] * identity * onsite[:, :, :, None, None, :]
    row_scale = jnp.exp(jax.random.uniform(keys[3], (NX, NY, NZ, 1, B, 1), jnp.float32, 0.0, 0.5 * math.log(10.0)))
    col_scale = jnp.exp(jax.random.uniform(keys[4], (NX, NY, NZ, 7, 1, B), jnp.float32, 0.0, 0.5 * math.log(10.0)))
    linear = (jnp.arange(NX)[:, None, None] * (NY * NZ) + jnp.arange(NY)[None, :, None] * NZ + jnp.arange(NZ)[None, None, :]).astype(jnp.float32) / (NX * NY * NZ - 1)
    amplitude = jnp.exp(0.5 * math.log(3.0) * linear)
    return matrix * row_scale * col_scale * amplitude[:, :, :, None, None, None]


def draw_keep_mask(key, part):
    drawn = jax.random.randint(key, (NX, NY, NZ, 7), 0, 4)
    keep = (drawn > 0).astype(jnp.int32)
    return keep.at[:, :, :, 0].set(1)


def setup_inputs(seed: int = 0) -> dict:
    arg_keys = jax.random.split(jax.random.key(seed), 3)
    hamiltonian = draw_hamiltonian(jax.random.fold_in(arg_keys[2], 71), 0)
    keep_mask = draw_keep_mask(jax.random.fold_in(arg_keys[2], 71), 0)
    return dict(hamiltonian=hamiltonian, keep_mask=keep_mask)


HIGHEST = lax.Precision.HIGHEST
OPPOSITE = (0, 2, 1, 4, 3, 6, 5)
TARGET_RMS = 1.0

def shifted(array, s):
    sign = 1 if s % 2 == 1 else -1
    return jnp.roll(array, -sign, (s - 1) // 2)

def block_mul(left, right):
    return jnp.einsum('xyzij,xyzjk->xyzik', left, right, precision=HIGHEST)

def product(left, right):
    left_self = left[:, :, :, 0]
    right_self = right[:, :, :, 0]
    centre = block_mul(left_self, right_self)
    others = []
    for s in range(1, 7):
        centre = centre + block_mul(left[:, :, :, s], shifted(right[:, :, :, OPPOSITE[s]], s))
        others.append(block_mul(left_self, right[:, :, :, s]) + block_mul(left[:, :, :, s], shifted(right_self, s)))
    return jnp.stack([centre] + others, axis=3)

def reference(hamiltonian, keep_mask):
    norm_sq = jnp.sum(hamiltonian * hamiltonian)
    factor = TARGET_RMS / jnp.sqrt(norm_sq / (NX * NY * NZ * B))
    iterate = factor * hamiltonian
    weights = keep_mask.astype(jnp.float32)[..., None, None]
    for sweep_index in range(ITERS):
        square = weights * product(iterate, iterate)
        cube = product(iterate, square)
        iterate = weights * (1.5 * iterate - 0.5 * cube)
    return iterate
```

```python
import functools

import jax
import jax.numpy as jnp
from jax import lax
from jax.experimental import pallas as pl
from jax.experimental.pallas import tpu as pltpu
from jax.sharding import PartitionSpec as P

MESH = pl.DeviceIdType.MESH
F32 = jnp.float32
BF16 = jnp.bfloat16
CHUNKS = 3


def kernel(
    sizes,
    count,
    h_hbm,
    keep,
    out,
    h,
    near_c,
    near_o,
    squares,
    near_keep,
    left,
    couple,
    first,
    tmp_a,
    tmp_b,
    kept_sum,
    centre,
    scale_sq,
    scale,
    part_x,
    part_y,
    part_z,
    load_sem,
    keep_send,
    keep_recv,
    part_send,
    part_recv,
    c_send,
    c_recv,
    o_send,
    o_recv,
    s_send,
    s_recv,
):
    nx, ny, nz = sizes
    width = h.shape[-1]
    rows = width // CHUNKS
    a, g, z = (lax.axis_index(n) for n in ("gx", "gy", "gz"))
    half = ny // 2
    at_top = lax.rem(g, half) == half - 1
    at_bottom = lax.rem(g, half) == 0
    edge = at_top | at_bottom
    up_x, down_x = lax.rem(a + 1, nx), lax.rem(a + nx - 1, nx)
    up_y, down_y = lax.rem(g + 1, ny), lax.rem(g + ny - 1, ny)
    up_z, down_z = lax.rem(z + 1, nz), lax.rem(z + nz - 1, nz)
    device = [
        (up_x, g, z),
        (down_x, g, z),
        (a, up_y, z),
        (a, down_y, z),
        (a, g, up_z),
        (a, g, down_z),
    ]
    across = nx - 1 - a
    cross = 1 - lax.rem(a, 2)
    near = 1 - cross
    passed_on = {2: (across, up_y, z), 3: (across, down_y, z)}
    wraps = {2: at_top, 3: at_bottom}

    def chunk(c):
        return pl.ds(c * rows, rows)

    barrier = pltpu.get_barrier_semaphore()
    peers_x = [(lax.rem(a + k, nx), g, z) for k in range(1, nx)]
    peers_y = [(a, lax.rem(g + k, ny), z) for k in range(1, ny)]
    peers_z = [(a, g, lax.rem(z + k, nz)) for k in range(1, nz)]
    for peer in peers_x + peers_y + peers_z:
        pl.semaphore_signal(barrier, inc=1, device_id=peer, device_id_type=MESH)
    for d in (2, 3):

        @pl.when(wraps[d])
        def _():
            pl.semaphore_signal(
                barrier, inc=1, device_id=passed_on[d], device_id_type=MESH
            )

    loads = [
        pltpu.make_async_copy(h_hbm.at[s], h.at[s], load_sem.at[s]) for s in range(7)
    ]
    for load in loads:
        load.start()
    total = jnp.zeros((8, 128), F32)
    for s in range(7):
        loads[s].wait()
        block = h[s]
        squared = jnp.sum((block * block).reshape(width // 8, 8, width), axis=0)
        for j in range(width // 128):
            total = total + squared[:, j * 128 : (j + 1) * 128]
    part_x[a] = total
    pl.semaphore_wait(barrier, nx + ny + nz - 3 + jnp.where(edge, 1, 0))

    def part_copies(stage, buffer, me, peers):
        return [
            pltpu.make_async_remote_copy(
                src_ref=buffer.at[me],
                dst_ref=buffer.at[me],
                send_sem=part_send.at[stage],
                recv_sem=part_recv.at[stage],
                device_id=peer,
                device_id_type=MESH,
            )
            for peer in peers
        ]

    def part_wait(stage, buffer, n):
        copy = pltpu.make_async_remote_copy(
            src_ref=buffer.at[pl.ds(0, n - 1)],
            dst_ref=buffer.at[pl.ds(0, n - 1)],
            send_sem=part_send.at[stage],
            recv_sem=part_recv.at[stage],
            device_id=device[0],
            device_id_type=MESH,
        )
        copy.wait_send()
        copy.wait_recv()

    def keep_copy(d):
        return pltpu.make_async_remote_copy(
            src_ref=keep.at[1 + d],
            dst_ref=near_keep.at[d ^ 1],
            send_sem=keep_send.at[d],
            recv_sem=keep_recv.at[d ^ 1],
            device_id=device[d],
            device_id_type=MESH,
        )

    def couple_copy(d):
        return pltpu.make_async_remote_copy(
            src_ref=h_hbm.at[1 + d],
            dst_ref=near_c.at[d ^ 1],
            send_sem=c_send.at[d],
            recv_sem=c_recv.at[d ^ 1],
            device_id=device[d],
            device_id_type=MESH,
        )

    def own_copy(d, c, source, target, send, recv):
        return pltpu.make_async_remote_copy(
            src_ref=source.at[0, chunk(c)],
            dst_ref=target.at[1 + (d ^ 1), chunk(c)],
            send_sem=send.at[d, c],
            recv_sem=recv.at[d ^ 1, c],
            device_id=device[d],
            device_id_type=MESH,
        )

    def pass_copy(d, c, target, send, recv):
        return pltpu.make_async_remote_copy(
            src_ref=target.at[1 + cross, chunk(c)],
            dst_ref=target.at[1 + (d ^ 1), chunk(c)],
            send_sem=send.at[d, c],
            recv_sem=recv.at[d ^ 1, c],
            device_id=passed_on[d],
            device_id_type=MESH,
        )

    def arrival(d, c, target, send, recv):
        return pltpu.make_async_remote_copy(
            src_ref=target.at[1 + d, chunk(c)],
            dst_ref=target.at[1 + d, chunk(c)],
            send_sem=send.at[0, c],
            recv_sem=recv.at[d, c],
            device_id=device[0],
            device_id_type=MESH,
        )

    def send_own(source, target, send, recv):
        for c in range(CHUNKS):
            for d in range(6):
                copy = own_copy(d, c, source, target, send, recv)
                if d in wraps:
                    pl.when(jnp.logical_not(wraps[d]))(copy.start)
                else:
                    copy.start()

    def pass_chunk(c, target, send, recv):
        arrival(cross, c, target, send, recv).wait_recv()
        for d in (2, 3):
            pl.when(wraps[d])(pass_copy(d, c, target, send, recv).start)

    squares_copies = (squares, squares, s_send, s_recv)
    own_copies = (h_hbm, near_o, o_send, o_recv)

    stage_x = part_copies(0, part_x, a, peers_x)
    for copy in stage_x:
        copy.start()
    for d in range(6):
        keep_copy(d).start()
    for d in range(6):
        couple_copy(d).start()
    send_own(*own_copies)

    def parts(x):
        high = x.astype(BF16)
        return high, (x - high.astype(F32)).astype(BF16)

    def as_left(x, ref):
        for c in range(CHUNKS):
            high, low = parts(x[:, c * rows : (c + 1) * rows])
            base = 3 * c * rows
            ref[:, base : base + rows] = high
            ref[:, base + rows : base + 2 * rows] = high
            ref[:, base + 2 * rows : base + 3 * rows] = low

    def as_right_chunk(x, ref, base):
        high, low = parts(x)
        ref[pl.ds(base, rows)] = high
        ref[pl.ds(base + rows, rows)] = low
        ref[pl.ds(base + 2 * rows, rows)] = high

    def as_right(x, ref):
        for c in range(CHUNKS):
            as_right_chunk(x[c * rows : (c + 1) * rows], ref, 3 * c * rows)

    def mul(x, y):
        return jnp.dot(x, y, preferred_element_type=F32)

    as_left(h[0], left.at[0])
    as_right(h[0], first)

    @pl.loop(0, 7)
    def _(s):
        block = h[s]
        as_left(block, left.at[s])
        as_right(block, tmp_b)
        out[s] = mul(left[0], tmp_b[...])

    part_wait(0, part_x, nx)
    part_y[g] = jnp.sum(part_x[...], axis=0)
    for copy in part_copies(1, part_y, g, peers_y):
        copy.start()
    part_wait(1, part_y, ny)
    part_z[z] = jnp.sum(part_y[...], axis=0)
    for copy in part_copies(2, part_z, z, peers_z):
        copy.start()

    kept_sum[...] = jnp.zeros_like(kept_sum)
    for d in range(6):
        keep_copy(d).wait_recv()

    @pl.loop(0, 6)
    def _(p):
        d = jnp.where(p == 0, near, jnp.where(p == 5, cross, jnp.where(p < 3, p + 3, p - 1)))
        pltpu.make_async_remote_copy(
            src_ref=near_c.at[d],
            dst_ref=near_c.at[d],
            send_sem=c_send.at[0],
            recv_sem=c_recv.at[d],
            device_id=device[0],
            device_id_type=MESH,
        ).wait_recv()
        as_right(near_c[d], couple.at[d])
        both = mul(left[1 + d], couple[d])
        out[0] += both
        kept_sum[...] += near_keep[d, 0:1] * both

    part_wait(2, part_z, nz)
    norm = jnp.sum(jnp.sum(part_z[...], axis=0), keepdims=True)
    norm = jnp.broadcast_to(norm, (8, width)) / count
    factor_sq = 1.0 / norm
    factor = 1.0 / jnp.sqrt(norm)
    scale_sq[...] = factor_sq
    for s in range(7):
        scale[s] = factor * keep[s]
    squares[0] = (scale_sq[0:1] * keep[0, 0:1]) * out[0]
    send_own(*squares_copies)

    for c in range(CHUNKS):
        pass_chunk(c, near_o, o_send, o_recv)
    as_left(scale_sq[0:1] * kept_sum[...], tmp_a)
    centre[...] = mul(tmp_a[...], first[...])
    as_right(squares[0], tmp_b)
    centre[...] += mul(left[0], tmp_b[...])

    @pl.loop(0, 6)
    def _(p):
        d = jnp.where(p == 0, near, jnp.where(p == 1, cross, jnp.where(p < 4, p + 2, p - 2)))

        @pl.when(p != 1)
        def _():
            for c in range(CHUNKS):
                arrival(d, c, near_o, o_send, o_recv).wait_recv()

        as_right(near_o[1 + d], tmp_b)
        with_own = mul(left[1 + d], tmp_b[...])
        as_right((scale_sq[0:1] * keep[1 + d, 0:1]) * (out[1 + d] + with_own), tmp_b)
        as_left((scale_sq[0:1] * near_keep[d, 0:1]) * with_own, tmp_a)
        out[1 + d] = scale[1 + d, 0:1] * (1.5 * h[1 + d] - 0.5 * mul(left[0], tmp_b[...]))
        centre[...] += mul(tmp_a[...], couple[d])

    out[0] = scale[0, 0:1] * (1.5 * h[0] - 0.5 * centre[...])

    def finish(d, c):
        base = 3 * c * rows
        as_right_chunk(squares[1 + d, chunk(c)], tmp_b, base)
        out[1 + d] -= (0.5 * scale[1 + d, 0:1]) * mul(
            left[1 + d, :, base : base + 3 * rows], tmp_b[base : base + 3 * rows]
        )

    def finish_y(c):
        @pl.loop(2, 4)
        def _(d):
            arrival(d, c, squares, s_send, s_recv).wait_recv()
            finish(d, c)

    for c in range(CHUNKS):
        pass_chunk(c, squares, s_send, s_recv)

        @pl.loop(0, 4)
        def _(p):
            d = jnp.where(p == 0, near, jnp.where(p == 1, cross, p + 2))

            @pl.when(p != 1)
            def _():
                arrival(d, c, squares, s_send, s_recv).wait_recv()

            finish(d, c)

        if c > 0:
            finish_y(c - 1)
    finish_y(CHUNKS - 1)

    for d in range(6):
        keep_copy(d).wait_send()
        couple_copy(d).wait_send()
        for c in range(CHUNKS):
            own_copy(d, c, *own_copies).wait_send()
            own_copy(d, c, *squares_copies).wait_send()


def body(hamiltonian, keep_mask):
    blocks = hamiltonian[0, 0, 0]
    width = blocks.shape[-1]
    sizes = tuple(lax.axis_size(n) for n in ("gx", "gy", "gz"))
    keep = jnp.broadcast_to(
        keep_mask[0, 0, 0].astype(F32)[:, None, None], (7, 8, width)
    )
    count = float(sizes[0] * sizes[1] * sizes[2] * width)
    square = (width, width)
    dma = pltpu.SemaphoreType.DMA
    vmem = pltpu.VMEM
    result = pl.pallas_call(
        functools.partial(kernel, sizes, count),
        out_shape=jax.ShapeDtypeStruct((7, *square), F32),
        in_specs=[
            pl.BlockSpec(memory_space=pltpu.HBM),
            pl.BlockSpec(memory_space=vmem),
        ],
        out_specs=pl.BlockSpec(memory_space=vmem),
        scratch_shapes=[
            vmem((7, *square), F32),
            vmem((6, *square), F32),
            vmem((7, *square), F32),
            vmem((7, *square), F32),
            vmem((6, 8, width), F32),
            vmem((7, width, 3 * width), BF16),
            vmem((6, 3 * width, width), BF16),
            vmem((3 * width, width), BF16),
            vmem((width, 3 * width), BF16),
            vmem((3 * width, width), BF16),
            vmem(square, F32),
            vmem(square, F32),
            vmem((8, width), F32),
            vmem((7, 8, width), F32),
            vmem((sizes[0], 8, 128), F32),
            vmem((sizes[1], 8, 128), F32),
            vmem((sizes[2], 8, 128), F32),
            dma((7,)),
            dma((6,)),
            dma((6,)),
            dma((3,)),
            dma((3,)),
            dma((6,)),
            dma((6,)),
            dma((6, CHUNKS)),
            dma((6, CHUNKS)),
            dma((6, CHUNKS)),
            dma((6, CHUNKS)),
        ],
        compiler_params=pltpu.CompilerParams(
            collective_id=0, has_side_effects=True, vmem_limit_bytes=56 << 20
        ),
        name="sign_step",
    )(blocks, keep)
    return result[None, None, None]


def solution(mesh):
    placed = (P("gx", "gy", "gz", None, None, None), P("gx", "gy", "gz", None))
    return jax.shard_map(
        body,
        mesh=mesh,
        in_specs=placed,
        out_specs=P("gx", "gy", "gz", None, None, None),
        check_vma=False,
    )
```

```python
import functools

import jax
import jax.numpy as jnp
from jax import lax
from jax.experimental import pallas as pl
from jax.experimental.pallas import tpu as pltpu
from jax.sharding import PartitionSpec as P

MESH = pl.DeviceIdType.MESH
F32 = jnp.float32
BF16 = jnp.bfloat16
CHUNKS = 3


def kernel(
    sizes,
    count,
    h_hbm,
    keep_in,
    out,
    h,
    near_c,
    near_o,
    squares,
    keep,
    near_keep,
    left,
    couple,
    first,
    tmp_a,
    tmp_b,
    kept_sum,
    centre,
    scale_sq,
    scale,
    part_x,
    part_y,
    part_z,
    load_sem,
    keep_send,
    keep_recv,
    part_send,
    part_recv,
    c_send,
    c_recv,
    o_send,
    o_recv,
    s_send,
    s_recv,
):
    nx, ny, nz = sizes
    width = h.shape[-1]
    rows = width // CHUNKS
    a, g, z = (lax.axis_index(n) for n in ("gx", "gy", "gz"))
    half = ny // 2
    at_top = lax.rem(g, half) == half - 1
    at_bottom = lax.rem(g, half) == 0
    edge = at_top | at_bottom
    up_x, down_x = lax.rem(a + 1, nx), lax.rem(a + nx - 1, nx)
    up_y, down_y = lax.rem(g + 1, ny), lax.rem(g + ny - 1, ny)
    up_z, down_z = lax.rem(z + 1, nz), lax.rem(z + nz - 1, nz)
    device = [
        (up_x, g, z),
        (down_x, g, z),
        (a, up_y, z),
        (a, down_y, z),
        (a, g, up_z),
        (a, g, down_z),
    ]
    across = nx - 1 - a
    cross = 1 - lax.rem(a, 2)
    near = 1 - cross
    passed_on = {2: (across, up_y, z), 3: (across, down_y, z)}
    wraps = {2: at_top, 3: at_bottom}

    def chunk(c):
        return pl.ds(c * rows, rows)

    barrier = pltpu.get_barrier_semaphore()
    peers_x = [(lax.rem(a + k, nx), g, z) for k in range(1, nx)]
    peers_y = [(a, lax.rem(g + k, ny), z) for k in range(1, ny)]
    peers_z = [(a, g, lax.rem(z + k, nz)) for k in range(1, nz)]
    for peer in peers_x + peers_y + peers_z:
        pl.semaphore_signal(barrier, inc=1, device_id=peer, device_id_type=MESH)
    for d in (2, 3):

        @pl.when(wraps[d])
        def _():
            pl.semaphore_signal(
                barrier, inc=1, device_id=passed_on[d], device_id_type=MESH
            )

    loads = [
        pltpu.make_async_copy(h_hbm.at[s], h.at[s], load_sem.at[s]) for s in range(7)
    ]
    for load in loads:
        load.start()
    for s in range(7):
        keep[s] = jnp.full((8, width), keep_in[s].astype(F32))
    total = jnp.zeros((8, 128), F32)
    for s in range(7):
        loads[s].wait()
        block = h[s]
        squared = jnp.sum((block * block).reshape(width // 8, 8, width), axis=0)
        for j in range(width // 128):
            total = total + squared[:, j * 128 : (j + 1) * 128]
    part_x[a] = total
    pl.semaphore_wait(barrier, nx + ny + nz - 3 + jnp.where(edge, 1, 0))

    def part_copies(stage, buffer, me, peers):
        return [
            pltpu.make_async_remote_copy(
                src_ref=buffer.at[me],
                dst_ref=buffer.at[me],
                send_sem=part_send.at[stage],
                recv_sem=part_recv.at[stage],
                device_id=peer,
                device_id_type=MESH,
            )
            for peer in peers
        ]

    def part_wait(stage, buffer, n):
        copy = pltpu.make_async_remote_copy(
            src_ref=buffer.at[pl.ds(0, n - 1)],
            dst_ref=buffer.at[pl.ds(0, n - 1)],
            send_sem=part_send.at[stage],
            recv_sem=part_recv.at[stage],
            device_id=device[0],
            device_id_type=MESH,
        )
        copy.wait_send()
        copy.wait_recv()

    def keep_copy(d):
        return pltpu.make_async_remote_copy(
            src_ref=keep.at[1 + d],
            dst_ref=near_keep.at[d ^ 1],
            send_sem=keep_send.at[d],
            recv_sem=keep_recv.at[d ^ 1],
            device_id=device[d],
            device_id_type=MESH,
        )

    def couple_copy(d):
        return pltpu.make_async_remote_copy(
            src_ref=h_hbm.at[1 + d],
            dst_ref=near_c.at[d ^ 1],
            send_sem=c_send.at[d],
            recv_sem=c_recv.at[d ^ 1],
            device_id=device[d],
            device_id_type=MESH,
        )

    def own_copy(d, c, source, target, send, recv):
        return pltpu.make_async_remote_copy(
            src_ref=source.at[0, chunk(c)],
            dst_ref=target.at[1 + (d ^ 1), chunk(c)],
            send_sem=send.at[d, c],
            recv_sem=recv.at[d ^ 1, c],
            device_id=device[d],
            device_id_type=MESH,
        )

    def pass_copy(d, c, target, send, recv):
        return pltpu.make_async_remote_copy(
            src_ref=target.at[1 + cross, chunk(c)],
            dst_ref=target.at[1 + (d ^ 1), chunk(c)],
            send_sem=send.at[d, c],
            recv_sem=recv.at[d ^ 1, c],
            device_id=passed_on[d],
            device_id_type=MESH,
        )

    def arrival(d, c, target, send, recv):
        return pltpu.make_async_remote_copy(
            src_ref=target.at[1 + d, chunk(c)],
            dst_ref=target.at[1 + d, chunk(c)],
            send_sem=send.at[0, c],
            recv_sem=recv.at[d, c],
            device_id=device[0],
            device_id_type=MESH,
        )

    def send_own(source, target, send, recv, directions=range(6)):
        for c in range(CHUNKS):
            for d in directions:
                copy = own_copy(d, c, source, target, send, recv)
                if d in wraps:
                    pl.when(jnp.logical_not(wraps[d]))(copy.start)
                else:
                    copy.start()

    def pass_chunk(c, target, send, recv):
        arrival(cross, c, target, send, recv).wait_recv()
        for d in (2, 3):
            pl.when(wraps[d])(pass_copy(d, c, target, send, recv).start)

    squares_copies = (squares, squares, s_send, s_recv)
    own_copies = (h_hbm, near_o, o_send, o_recv)

    def parts(x):
        high = x.astype(BF16)
        return high, (x - high.astype(F32)).astype(BF16)

    def as_left(x, ref):
        for c in range(CHUNKS):
            high, low = parts(x[:, c * rows : (c + 1) * rows])
            base = 3 * c * rows
            ref[:, base : base + rows] = high
            ref[:, base + rows : base + 2 * rows] = high
            ref[:, base + 2 * rows : base + 3 * rows] = low

    def as_right_chunk(x, ref, base):
        high, low = parts(x)
        ref[pl.ds(base, rows)] = high
        ref[pl.ds(base + rows, rows)] = low
        ref[pl.ds(base + 2 * rows, rows)] = high

    def as_right(x, ref):
        for c in range(CHUNKS):
            as_right_chunk(x[c * rows : (c + 1) * rows], ref, 3 * c * rows)

    def mul(x, y):
        return jnp.dot(x, y, preferred_element_type=F32)

    as_left(h[0], left.at[0])
    as_right(h[0], first)

    def own_products(low, high):
        @pl.loop(low, high)
        def _(s):
            block = h[s]
            as_left(block, left.at[s])
            as_right(block, tmp_b)
            out[s] = mul(left[0], tmp_b[...])

    def send_parts(stage, buffer, me, peers):
        for copy in part_copies(stage, buffer, me, peers):
            copy.start()

    def send_couples(*directions):
        for d in directions:
            keep_copy(d).start()
        for d in directions:
            couple_copy(d).start()

    send_parts(0, part_x, a, peers_x)
    send_couples(0, 1)
    own_products(0, 2)
    part_wait(0, part_x, nx)
    part_y[g] = jnp.sum(part_x[...], axis=0)
    send_parts(1, part_y, g, peers_y)
    send_couples(2, 3)
    own_products(2, 4)
    part_wait(1, part_y, ny)
    part_z[z] = jnp.sum(part_y[...], axis=0)
    send_parts(2, part_z, z, peers_z)
    send_couples(4, 5)
    send_own(*own_copies)
    own_products(4, 7)

    kept_sum[...] = jnp.zeros_like(kept_sum)
    for d in range(6):
        keep_copy(d).wait_recv()

    @pl.loop(0, 6)
    def _(p):
        d = jnp.where(p == 0, near, jnp.where(p == 5, cross, jnp.where(p < 3, p + 3, p - 1)))
        pltpu.make_async_remote_copy(
            src_ref=near_c.at[d],
            dst_ref=near_c.at[d],
            send_sem=c_send.at[0],
            recv_sem=c_recv.at[d],
            device_id=device[0],
            device_id_type=MESH,
        ).wait_recv()
        as_right(near_c[d], couple.at[d])
        both = mul(left[1 + d], couple[d])
        out[0] += both
        kept_sum[...] += near_keep[d, 0:1] * both

    part_wait(2, part_z, nz)
    norm = jnp.sum(jnp.sum(part_z[...], axis=0), keepdims=True)
    norm = jnp.broadcast_to(norm, (8, width)) / count
    factor_sq = 1.0 / norm
    factor = 1.0 / jnp.sqrt(norm)
    scale_sq[...] = factor_sq
    for s in range(7):
        scale[s] = factor * keep[s]
    squares[0] = (scale_sq[0:1] * keep[0, 0:1]) * out[0]
    send_own(*squares_copies)

    for c in range(CHUNKS):
        pass_chunk(c, near_o, o_send, o_recv)
    as_left(scale_sq[0:1] * kept_sum[...], tmp_a)
    centre[...] = mul(tmp_a[...], first[...])
    as_right(squares[0], tmp_b)
    centre[...] += mul(left[0], tmp_b[...])

    def others(low, high):
        @pl.loop(low, high)
        def _(p):
            d = jnp.where(p == 0, near, jnp.where(p == 3, cross, jnp.where(p < 3, p + 3, p - 2)))

            @pl.when(p != 3)
            def _():
                for c in range(CHUNKS):
                    arrival(d, c, near_o, o_send, o_recv).wait_recv()

            as_right(near_o[1 + d], tmp_b)
            with_own = mul(left[1 + d], tmp_b[...])
            as_right((scale_sq[0:1] * keep[1 + d, 0:1]) * (out[1 + d] + with_own), tmp_b)
            as_left((scale_sq[0:1] * near_keep[d, 0:1]) * with_own, tmp_a)
            out[1 + d] = scale[1 + d, 0:1] * (
                1.5 * h[1 + d] - 0.5 * mul(left[0], tmp_b[...])
            )
            centre[...] += mul(tmp_a[...], couple[d])

    others(0, 4)
    for c in range(CHUNKS):
        pass_chunk(c, squares, s_send, s_recv)
        if c < 2:
            others(4 + c, 5 + c)
    out[0] = scale[0, 0:1] * (1.5 * h[0] - 0.5 * centre[...])

    def finish(d, c):
        base = 3 * c * rows
        as_right_chunk(squares[1 + d, chunk(c)], tmp_b, base)
        out[1 + d] -= (0.5 * scale[1 + d, 0:1]) * mul(
            left[1 + d, :, base : base + 3 * rows], tmp_b[base : base + 3 * rows]
        )

    for c in range(CHUNKS):

        @pl.loop(0, 4)
        def _(p):
            d = jnp.where(p == 0, near, jnp.where(p == 3, cross, p + 3))

            @pl.when(p != 3)
            def _():
                arrival(d, c, squares, s_send, s_recv).wait_recv()

            finish(d, c)

    for c in range(CHUNKS):

        @pl.loop(2, 4)
        def _(d):
            arrival(d, c, squares, s_send, s_recv).wait_recv()
            finish(d, c)

    for d in range(6):
        keep_copy(d).wait_send()
        couple_copy(d).wait_send()
        for c in range(CHUNKS):
            own_copy(d, c, *own_copies).wait_send()
            own_copy(d, c, *squares_copies).wait_send()


def write_out(result, out_hbm, sem):
    copies = [
        pltpu.make_async_copy(result.at[s], out_hbm.at[s], sem.at[s]) for s in range(7)
    ]
    for copy in copies:
        copy.start()
    for copy in copies:
        copy.wait()


def body(hamiltonian, keep_mask):
    blocks = hamiltonian[0, 0, 0]
    width = blocks.shape[-1]
    sizes = tuple(lax.axis_size(n) for n in ("gx", "gy", "gz"))
    keep = keep_mask[0, 0, 0]
    count = float(sizes[0] * sizes[1] * sizes[2] * width)
    square = (width, width)
    dma = pltpu.SemaphoreType.DMA
    vmem = pltpu.VMEM
    result = pl.pallas_call(
        functools.partial(kernel, sizes, count),
        out_shape=vmem((7, *square), F32),
        in_specs=[
            pl.BlockSpec(memory_space=pltpu.HBM),
            pl.BlockSpec(memory_space=pltpu.SMEM),
        ],
        out_specs=pl.BlockSpec(memory_space=vmem),
        scratch_shapes=[
            vmem((7, *square), F32),
            vmem((6, *square), F32),
            vmem((7, *square), F32),
            vmem((7, *square), F32),
            vmem((7, 8, width), F32),
            vmem((6, 8, width), F32),
            vmem((7, width, 3 * width), BF16),
            vmem((6, 3 * width, width), BF16),
            vmem((3 * width, width), BF16),
            vmem((width, 3 * width), BF16),
            vmem((3 * width, width), BF16),
            vmem(square, F32),
            vmem(square, F32),
            vmem((8, width), F32),
            vmem((7, 8, width), F32),
            vmem((sizes[0], 8, 128), F32),
            vmem((sizes[1], 8, 128), F32),
            vmem((sizes[2], 8, 128), F32),
            dma((7,)),
            dma((6,)),
            dma((6,)),
            dma((3,)),
            dma((3,)),
            dma((6,)),
            dma((6,)),
            dma((6, CHUNKS)),
            dma((6, CHUNKS)),
            dma((6, CHUNKS)),
            dma((6, CHUNKS)),
        ],
        compiler_params=pltpu.CompilerParams(
            collective_id=0, has_side_effects=True, vmem_limit_bytes=56 << 20
        ),
        name="sign_step",
    )(blocks, keep)
    result = pl.pallas_call(
        write_out,
        out_shape=jax.ShapeDtypeStruct((7, *square), F32),
        in_specs=[pl.BlockSpec(memory_space=vmem)],
        out_specs=pl.BlockSpec(memory_space=pltpu.HBM),
        scratch_shapes=[dma((7,))],
        compiler_params=pltpu.CompilerParams(vmem_limit_bytes=6 << 20),
        name="write_out",
    )(result)
    return result[None, None, None]


def solution(mesh):
    placed = (P("gx", "gy", "gz", None, None, None), P("gx", "gy", "gz", None))
    return jax.shard_map(
        body,
        mesh=mesh,
        in_specs=placed,
        out_specs=P("gx", "gy", "gz", None, None, None),
        check_vma=False,
    )
```

```python
import functools

import jax
import jax.numpy as jnp
from jax import lax
from jax.experimental import pallas as pl
from jax.experimental.pallas import tpu as pltpu
from jax.sharding import PartitionSpec as P

MESH = pl.DeviceIdType.MESH
F32 = jnp.float32
BF16 = jnp.bfloat16
CHUNKS = 3


def kernel(
    sizes,
    count,
    h_hbm,
    keep_in,
    out,
    h,
    near_c,
    near_o,
    squares,
    keep,
    near_keep,
    left,
    couple,
    first,
    tmp_a,
    tmp_b,
    kept_sum,
    centre,
    scale_sq,
    scale,
    part_x,
    part_y,
    part_z,
    load_sem,
    keep_send,
    keep_recv,
    part_send,
    part_recv,
    c_send,
    c_recv,
    o_send,
    o_recv,
    s_send,
    s_recv,
):
    nx, ny, nz = sizes
    width = h.shape[-1]
    rows = width // CHUNKS
    a, g, z = (lax.axis_index(n) for n in ("gx", "gy", "gz"))
    half = ny // 2
    at_top = lax.rem(g, half) == half - 1
    at_bottom = lax.rem(g, half) == 0
    edge = at_top | at_bottom
    up_x, down_x = lax.rem(a + 1, nx), lax.rem(a + nx - 1, nx)
    up_y, down_y = lax.rem(g + 1, ny), lax.rem(g + ny - 1, ny)
    up_z, down_z = lax.rem(z + 1, nz), lax.rem(z + nz - 1, nz)
    device = [
        (up_x, g, z),
        (down_x, g, z),
        (a, up_y, z),
        (a, down_y, z),
        (a, g, up_z),
        (a, g, down_z),
    ]
    across = nx - 1 - a
    cross = 1 - lax.rem(a, 2)
    near = 1 - cross
    passed_on = {2: (across, up_y, z), 3: (across, down_y, z)}
    wraps = {2: at_top, 3: at_bottom}

    def chunk(c):
        return pl.ds(pl.multiple_of(c * rows, rows), rows)

    barrier = pltpu.get_barrier_semaphore()
    peers_x = [(lax.rem(a + k, nx), g, z) for k in range(1, nx)]
    peers_y = [(a, lax.rem(g + k, ny), z) for k in range(1, ny)]
    peers_z = [(a, g, lax.rem(z + k, nz)) for k in range(1, nz)]
    for peer in peers_x + peers_y + peers_z:
        pl.semaphore_signal(barrier, inc=1, device_id=peer, device_id_type=MESH)
    for d in (2, 3):

        @pl.when(wraps[d])
        def _():
            pl.semaphore_signal(
                barrier, inc=1, device_id=passed_on[d], device_id_type=MESH
            )

    loads = [
        pltpu.make_async_copy(h_hbm.at[s], h.at[s], load_sem.at[s]) for s in range(7)
    ]
    for load in loads:
        load.start()
    for s in range(7):
        keep[s] = jnp.full((8, width), keep_in[s].astype(F32))
    total = jnp.zeros((8, 128), F32)
    for s in range(7):
        loads[s].wait()
        block = h[s]
        squared = jnp.sum((block * block).reshape(width // 8, 8, width), axis=0)
        for j in range(width // 128):
            total = total + squared[:, j * 128 : (j + 1) * 128]
    part_x[a] = total
    pl.semaphore_wait(barrier, nx + ny + nz - 3 + jnp.where(edge, 1, 0))

    def part_copies(stage, buffer, me, peers):
        return [
            pltpu.make_async_remote_copy(
                src_ref=buffer.at[me],
                dst_ref=buffer.at[me],
                send_sem=part_send.at[stage],
                recv_sem=part_recv.at[stage],
                device_id=peer,
                device_id_type=MESH,
            )
            for peer in peers
        ]

    def part_wait(stage, buffer, n):
        copy = pltpu.make_async_remote_copy(
            src_ref=buffer.at[pl.ds(0, n - 1)],
            dst_ref=buffer.at[pl.ds(0, n - 1)],
            send_sem=part_send.at[stage],
            recv_sem=part_recv.at[stage],
            device_id=device[0],
            device_id_type=MESH,
        )
        copy.wait_send()
        copy.wait_recv()

    def keep_copy(d):
        return pltpu.make_async_remote_copy(
            src_ref=keep.at[1 + d],
            dst_ref=near_keep.at[d ^ 1],
            send_sem=keep_send.at[d],
            recv_sem=keep_recv.at[d ^ 1],
            device_id=device[d],
            device_id_type=MESH,
        )

    def couple_copy(d):
        return pltpu.make_async_remote_copy(
            src_ref=h_hbm.at[1 + d],
            dst_ref=near_c.at[d ^ 1],
            send_sem=c_send.at[d],
            recv_sem=c_recv.at[d ^ 1],
            device_id=device[d],
            device_id_type=MESH,
        )

    def own_copy(d, c, source, target, send, recv):
        return pltpu.make_async_remote_copy(
            src_ref=source.at[0, chunk(c)],
            dst_ref=target.at[1 + (d ^ 1), chunk(c)],
            send_sem=send.at[d, c],
            recv_sem=recv.at[d ^ 1, c],
            device_id=device[d],
            device_id_type=MESH,
        )

    def pass_copy(d, c, target, send, recv):
        return pltpu.make_async_remote_copy(
            src_ref=target.at[1 + cross, chunk(c)],
            dst_ref=target.at[1 + (d ^ 1), chunk(c)],
            send_sem=send.at[d, c],
            recv_sem=recv.at[d ^ 1, c],
            device_id=passed_on[d],
            device_id_type=MESH,
        )

    def arrival(d, c, target, send, recv):
        return pltpu.make_async_remote_copy(
            src_ref=target.at[1 + d, chunk(c)],
            dst_ref=target.at[1 + d, chunk(c)],
            send_sem=send.at[0, c],
            recv_sem=recv.at[d, c],
            device_id=device[0],
            device_id_type=MESH,
        )

    def send_own(source, target, send, recv, directions=range(6)):
        for c in range(CHUNKS):
            for d in directions:
                copy = own_copy(d, c, source, target, send, recv)
                if d in wraps:
                    pl.when(jnp.logical_not(wraps[d]))(copy.start)
                else:
                    copy.start()

    def pass_chunk(c, target, send, recv):
        arrival(cross, c, target, send, recv).wait_recv()
        for d in (2, 3):
            pl.when(wraps[d])(pass_copy(d, c, target, send, recv).start)

    squares_copies = (squares, squares, s_send, s_recv)
    own_copies = (h_hbm, near_o, o_send, o_recv)

    def parts(x):
        high = x.astype(BF16)
        return high, (x - high.astype(F32)).astype(BF16)

    def as_left(x, ref):
        for c in range(CHUNKS):
            high, low = parts(x[:, c * rows : (c + 1) * rows])
            base = 3 * c * rows
            ref[:, base : base + rows] = high
            ref[:, base + rows : base + 2 * rows] = high
            ref[:, base + 2 * rows : base + 3 * rows] = low

    def as_right_chunk(x, ref, base):
        high, low = parts(x)
        ref[pl.ds(base, rows)] = high
        ref[pl.ds(base + rows, rows)] = low
        ref[pl.ds(base + 2 * rows, rows)] = high

    def as_right(x, ref):
        for c in range(CHUNKS):
            as_right_chunk(x[c * rows : (c + 1) * rows], ref, 3 * c * rows)

    def mul(x, y):
        return jnp.dot(x, y, preferred_element_type=F32)

    as_left(h[0], left.at[0])
    as_right(h[0], first)

    def send_parts(stage, buffer, me, peers):
        for copy in part_copies(stage, buffer, me, peers):
            copy.start()

    def send_couples(*directions):
        for d in directions:
            keep_copy(d).start()
        for d in directions:
            couple_copy(d).start()

    send_parts(0, part_x, a, peers_x)
    send_couples(0, 1, 2, 3)

    @pl.loop(0, 7)
    def _(s):
        @pl.when(s == 1)
        def _():
            part_wait(0, part_x, nx)
            part_z[z] = jnp.sum(part_x[...], axis=0)
            send_parts(1, part_z, z, peers_z)
            send_couples(4, 5)

        @pl.when(s == 4)
        def _():
            part_wait(1, part_z, nz)
            part_y[g] = jnp.sum(part_z[...], axis=0)
            send_parts(2, part_y, g, peers_y)
            send_own(*own_copies)

        block = h[s]
        as_left(block, left.at[s])
        as_right(block, tmp_b)
        out[s] = mul(left[0], tmp_b[...])

    kept_sum[...] = jnp.zeros_like(kept_sum)
    centre[...] = jnp.zeros_like(centre)
    for d in range(6):
        keep_copy(d).wait_recv()

    @pl.loop(0, 6)
    def _(p):
        d = jnp.where(p == 0, near, jnp.where(p == 5, cross, jnp.where(p < 3, p + 3, p - 1)))
        pltpu.make_async_remote_copy(
            src_ref=near_c.at[d],
            dst_ref=near_c.at[d],
            send_sem=c_send.at[0],
            recv_sem=c_recv.at[d],
            device_id=device[0],
            device_id_type=MESH,
        ).wait_recv()
        as_right(near_c[d], couple.at[d])
        both = mul(left[1 + d], couple[d])
        out[0] += both
        kept_sum[...] += near_keep[d, 0:1] * both

    squares[0] = keep[0, 0:1] * out[0]
    send_own(*squares_copies)

    part_wait(2, part_y, ny)
    norm = jnp.sum(jnp.sum(part_y[...], axis=0), keepdims=True)
    norm = jnp.broadcast_to(norm, (8, width)) / count
    factor = 1.0 / jnp.sqrt(norm)
    scale_sq[...] = 1.0 / norm
    for s in range(7):
        scale[s] = factor * keep[s]

    @pl.loop(0, 6)
    def _(p):
        d = jnp.where(p == 0, near, jnp.where(p == 3, cross, jnp.where(p < 3, p + 3, p - 2)))

        @pl.when(p == 2)
        def _():
            as_left(scale_sq[0:1] * kept_sum[...], tmp_a)
            centre[...] += mul(tmp_a[...], first[...])
            as_right(scale_sq[0:1] * squares[0], tmp_b)
            centre[...] += mul(left[0], tmp_b[...])

        @pl.when(p < CHUNKS)
        def _():
            pass_chunk(p, near_o, o_send, o_recv)

        @pl.when(p > 3)
        def _():
            pass_chunk(p - 4, squares, s_send, s_recv)

        @pl.when(p != 3)
        def _():
            for c in range(CHUNKS):
                arrival(d, c, near_o, o_send, o_recv).wait_recv()

        as_right(near_o[1 + d], tmp_b)
        with_own = mul(left[1 + d], tmp_b[...])
        as_right((scale_sq[0:1] * keep[1 + d, 0:1]) * (out[1 + d] + with_own), tmp_b)
        as_left((scale_sq[0:1] * near_keep[d, 0:1]) * with_own, tmp_a)
        out[1 + d] = scale[1 + d, 0:1] * (
            1.5 * h[1 + d] - 0.5 * mul(left[0], tmp_b[...])
        )
        centre[...] += mul(tmp_a[...], couple[d])

    @pl.loop(0, 4)
    def _(p):
        d = jnp.where(p == 0, near, jnp.where(p == 3, cross, p + 3))

        @pl.when(p == 1)
        def _():
            pass_chunk(CHUNKS - 1, squares, s_send, s_recv)
            out[0] = scale[0, 0:1] * (1.5 * h[0] - 0.5 * centre[...])

        @pl.when(p != 3)
        def _():
            for c in range(CHUNKS):
                arrival(d, c, squares, s_send, s_recv).wait_recv()

        as_right(scale_sq[0:1] * squares[1 + d], tmp_b)
        out[1 + d] -= (0.5 * scale[1 + d, 0:1]) * mul(left[1 + d], tmp_b[...])

    @pl.loop(0, 2 * CHUNKS)
    def _(q):
        d, c = 2 + lax.rem(q, 2), q // 2
        arrival(d, c, squares, s_send, s_recv).wait_recv()
        as_right_chunk(scale_sq[0:1] * squares[1 + d, chunk(c)], tmp_b, 0)
        columns = pl.ds(pl.multiple_of(3 * c * rows, 3 * rows), 3 * rows)
        out[1 + d] -= (0.5 * scale[1 + d, 0:1]) * mul(
            left[1 + d, :, columns], tmp_b[0 : 3 * rows]
        )

    for d in range(6):
        keep_copy(d).wait_send()
        couple_copy(d).wait_send()
        for c in range(CHUNKS):
            own_copy(d, c, *own_copies).wait_send()
            own_copy(d, c, *squares_copies).wait_send()


def write_out(result, out_hbm, sem):
    copies = [
        pltpu.make_async_copy(result.at[s], out_hbm.at[s], sem.at[s]) for s in range(7)
    ]
    for copy in copies:
        copy.start()
    for copy in copies:
        copy.wait()


def body(hamiltonian, keep_mask):
    blocks = hamiltonian[0, 0, 0]
    width = blocks.shape[-1]
    sizes = tuple(lax.axis_size(n) for n in ("gx", "gy", "gz"))
    keep = keep_mask[0, 0, 0]
    count = float(sizes[0] * sizes[1] * sizes[2] * width)
    square = (width, width)
    dma = pltpu.SemaphoreType.DMA
    vmem = pltpu.VMEM
    result = pl.pallas_call(
        functools.partial(kernel, sizes, count),
        out_shape=vmem((7, *square), F32),
        in_specs=[
            pl.BlockSpec(memory_space=pltpu.HBM),
            pl.BlockSpec(memory_space=pltpu.SMEM),
        ],
        out_specs=pl.BlockSpec(memory_space=vmem),
        scratch_shapes=[
            vmem((7, *square), F32),
            vmem((6, *square), F32),
            vmem((7, *square), F32),
            vmem((7, *square), F32),
            vmem((7, 8, width), F32),
            vmem((6, 8, width), F32),
            vmem((7, width, 3 * width), BF16),
            vmem((6, 3 * width, width), BF16),
            vmem((3 * width, width), BF16),
            vmem((width, 3 * width), BF16),
            vmem((3 * width, width), BF16),
            vmem(square, F32),
            vmem(square, F32),
            vmem((8, width), F32),
            vmem((7, 8, width), F32),
            vmem((sizes[0], 8, 128), F32),
            vmem((sizes[1], 8, 128), F32),
            vmem((sizes[2], 8, 128), F32),
            dma((7,)),
            dma((6,)),
            dma((6,)),
            dma((3,)),
            dma((3,)),
            dma((6,)),
            dma((6,)),
            dma((6, CHUNKS)),
            dma((6, CHUNKS)),
            dma((6, CHUNKS)),
            dma((6, CHUNKS)),
        ],
        compiler_params=pltpu.CompilerParams(
            collective_id=0, has_side_effects=True, vmem_limit_bytes=56 << 20
        ),
        name="sign_step",
    )(blocks, keep)
    result = pl.pallas_call(
        write_out,
        out_shape=jax.ShapeDtypeStruct((7, *square), F32),
        in_specs=[pl.BlockSpec(memory_space=vmem)],
        out_specs=pl.BlockSpec(memory_space=pltpu.HBM),
        scratch_shapes=[dma((7,))],
        compiler_params=pltpu.CompilerParams(vmem_limit_bytes=6 << 20),
        name="write_out",
    )(result)
    return result[None, None, None]


def solution(mesh):
    placed = (P("gx", "gy", "gz", None, None, None), P("gx", "gy", "gz", None))
    return jax.shard_map(
        body,
        mesh=mesh,
        in_specs=placed,
        out_specs=P("gx", "gy", "gz", None, None, None),
        check_vma=False,
    )
```

```python
import functools

import jax
import jax.numpy as jnp
from jax import lax
from jax.experimental import pallas as pl
from jax.experimental.pallas import tpu as pltpu
from jax.sharding import PartitionSpec as P

MESH = pl.DeviceIdType.MESH
F32 = jnp.float32
BF16 = jnp.bfloat16
CHUNKS = 3


def kernel(
    sizes,
    count,
    h_hbm,
    keep_in,
    out,
    h,
    near_c,
    near_o,
    squares,
    keep,
    near_keep,
    relay,
    left,
    couple,
    first,
    tmp_a,
    tmp_b,
    kept_sum,
    centre,
    scale_sq,
    scale,
    part_x,
    part_y,
    part_z,
    load_sem,
    keep_send,
    keep_recv,
    part_send,
    part_recv,
    c_send,
    c_recv,
    relay_send,
    relay_recv,
    o_send,
    o_recv,
    s_send,
    s_recv,
):
    nx, ny, nz = sizes
    width = h.shape[-1]
    rows = width // CHUNKS
    a, g, z = (lax.axis_index(n) for n in ("gx", "gy", "gz"))
    half = ny // 2
    at_top = lax.rem(g, half) == half - 1
    at_bottom = lax.rem(g, half) == 0
    edge = at_top | at_bottom
    up_x, down_x = lax.rem(a + 1, nx), lax.rem(a + nx - 1, nx)
    up_y, down_y = lax.rem(g + 1, ny), lax.rem(g + ny - 1, ny)
    up_z, down_z = lax.rem(z + 1, nz), lax.rem(z + nz - 1, nz)
    device = [
        (up_x, g, z),
        (down_x, g, z),
        (a, up_y, z),
        (a, down_y, z),
        (a, g, up_z),
        (a, g, down_z),
    ]
    across = nx - 1 - a
    cross = 1 - lax.rem(a, 2)
    near = 1 - cross
    passed_on = {2: (across, up_y, z), 3: (across, down_y, z)}
    wraps = {2: at_top, 3: at_bottom}
    even = lax.rem(a, 2) == 0
    relays = even & jnp.logical_not(edge)
    above = lax.rem(g, half) == half - 2
    relay_to = (a, lax.rem(g + jnp.where(above, 2, ny - 2), ny), z)

    def chunk(c):
        return pl.ds(pl.multiple_of(c * rows, rows), rows)

    barrier = pltpu.get_barrier_semaphore()
    peers_x = [(lax.rem(a + k, nx), g, z) for k in range(1, nx)]
    peers_y = [(a, lax.rem(g + k, ny), z) for k in range(1, ny)]
    peers_z = [(a, g, lax.rem(z + k, nz)) for k in range(1, nz)]
    for peer in peers_x + peers_y + peers_z:
        pl.semaphore_signal(barrier, inc=1, device_id=peer, device_id_type=MESH)
    for d in (2, 3):

        @pl.when(wraps[d])
        def _():
            pl.semaphore_signal(
                barrier, inc=1, device_id=passed_on[d], device_id_type=MESH
            )

    loads = [
        pltpu.make_async_copy(h_hbm.at[s], h.at[s], load_sem.at[s]) for s in range(7)
    ]
    for load in loads:
        load.start()
    for s in range(7):
        keep[s] = jnp.full((8, width), keep_in[s].astype(F32))
    total = jnp.zeros((8, 128), F32)
    for s in range(7):
        loads[s].wait()
        block = h[s]
        squared = jnp.sum((block * block).reshape(width // 8, 8, width), axis=0)
        for j in range(width // 128):
            total = total + squared[:, j * 128 : (j + 1) * 128]
    part_x[a] = total
    pl.semaphore_wait(barrier, nx + ny + nz - 3 + jnp.where(edge, 1, 0))

    def part_copies(stage, buffer, me, peers):
        return [
            pltpu.make_async_remote_copy(
                src_ref=buffer.at[me],
                dst_ref=buffer.at[me],
                send_sem=part_send.at[stage],
                recv_sem=part_recv.at[stage],
                device_id=peer,
                device_id_type=MESH,
            )
            for peer in peers
        ]

    def part_wait(stage, buffer, n):
        copy = pltpu.make_async_remote_copy(
            src_ref=buffer.at[pl.ds(0, n - 1)],
            dst_ref=buffer.at[pl.ds(0, n - 1)],
            send_sem=part_send.at[stage],
            recv_sem=part_recv.at[stage],
            device_id=device[0],
            device_id_type=MESH,
        )
        copy.wait_send()
        copy.wait_recv()

    def keep_copy(d):
        return pltpu.make_async_remote_copy(
            src_ref=keep.at[1 + d],
            dst_ref=near_keep.at[d ^ 1],
            send_sem=keep_send.at[d],
            recv_sem=keep_recv.at[d ^ 1],
            device_id=device[d],
            device_id_type=MESH,
        )

    def couple_copy(d):
        return pltpu.make_async_remote_copy(
            src_ref=h_hbm.at[1 + d],
            dst_ref=near_c.at[d ^ 1],
            send_sem=c_send.at[d],
            recv_sem=c_recv.at[d ^ 1],
            device_id=device[d],
            device_id_type=MESH,
        )

    def to_relay(d, c):
        return pltpu.make_async_remote_copy(
            src_ref=h_hbm.at[1 + d, chunk(c)],
            dst_ref=relay.at[chunk(c)],
            send_sem=c_send.at[d],
            recv_sem=relay_recv.at[c],
            device_id=device[d ^ 1],
            device_id_type=MESH,
        )

    def from_relay(c):
        return pltpu.make_async_remote_copy(
            src_ref=relay.at[chunk(c)],
            dst_ref=near_c.at[jnp.where(above, 3, 2), chunk(c)],
            send_sem=relay_send.at[0],
            recv_sem=c_recv.at[jnp.where(above, 3, 2)],
            device_id=relay_to,
            device_id_type=MESH,
        )

    def own_copy(d, c, source, target, send, recv):
        return pltpu.make_async_remote_copy(
            src_ref=source.at[0, chunk(c)],
            dst_ref=target.at[1 + (d ^ 1), chunk(c)],
            send_sem=send.at[d, c],
            recv_sem=recv.at[d ^ 1, c],
            device_id=device[d],
            device_id_type=MESH,
        )

    def pass_copy(d, c, target, send, recv):
        return pltpu.make_async_remote_copy(
            src_ref=target.at[1 + cross, chunk(c)],
            dst_ref=target.at[1 + (d ^ 1), chunk(c)],
            send_sem=send.at[d, c],
            recv_sem=recv.at[d ^ 1, c],
            device_id=passed_on[d],
            device_id_type=MESH,
        )

    def arrival(d, c, target, send, recv):
        return pltpu.make_async_remote_copy(
            src_ref=target.at[1 + d, chunk(c)],
            dst_ref=target.at[1 + d, chunk(c)],
            send_sem=send.at[0, c],
            recv_sem=recv.at[d, c],
            device_id=device[0],
            device_id_type=MESH,
        )

    def send_own(source, target, send, recv, directions=range(6)):
        for c in range(CHUNKS):
            for d in directions:
                copy = own_copy(d, c, source, target, send, recv)
                if d in wraps:
                    pl.when(jnp.logical_not(wraps[d]))(copy.start)
                else:
                    copy.start()

    def pass_chunk(c, target, send, recv):
        arrival(cross, c, target, send, recv).wait_recv()
        for d in (2, 3):
            pl.when(wraps[d])(pass_copy(d, c, target, send, recv).start)

    squares_copies = (squares, squares, s_send, s_recv)
    own_copies = (h_hbm, near_o, o_send, o_recv)

    def parts(x):
        high = x.astype(BF16)
        return high, (x - high.astype(F32)).astype(BF16)

    def as_left(x, ref):
        for c in range(CHUNKS):
            high, low = parts(x[:, c * rows : (c + 1) * rows])
            base = 3 * c * rows
            ref[:, base : base + rows] = high
            ref[:, base + rows : base + 2 * rows] = high
            ref[:, base + 2 * rows : base + 3 * rows] = low

    def as_right_chunk(x, ref, base):
        high, low = parts(x)
        ref[pl.ds(base, rows)] = high
        ref[pl.ds(base + rows, rows)] = low
        ref[pl.ds(base + 2 * rows, rows)] = high

    def as_right(x, ref):
        for c in range(CHUNKS):
            as_right_chunk(x[c * rows : (c + 1) * rows], ref, 3 * c * rows)

    def mul(x, y):
        return jnp.dot(x, y, preferred_element_type=F32)

    as_left(h[0], left.at[0])
    as_right(h[0], first)

    def send_parts(stage, buffer, me, peers):
        for copy in part_copies(stage, buffer, me, peers):
            copy.start()

    def send_couples(*directions):
        for d in directions:
            keep_copy(d).start()
        for d in directions:
            if d in wraps:

                @pl.when(wraps[d] & even)
                def _():
                    for c in range(CHUNKS):
                        to_relay(d, c).start()

                pl.when(wraps[d] & jnp.logical_not(even))(couple_copy(d).start)
        for d in directions:
            if d in wraps:
                pl.when(jnp.logical_not(wraps[d]))(couple_copy(d).start)
            else:
                couple_copy(d).start()

    send_parts(0, part_x, a, peers_x)
    send_couples(0, 1, 2, 3)

    @pl.loop(0, 7)
    def _(s):
        @pl.when(s == 1)
        def _():
            part_wait(0, part_x, nx)
            part_z[z] = jnp.sum(part_x[...], axis=0)
            send_parts(1, part_z, z, peers_z)
            send_couples(4, 5)

        @pl.when(s == 4)
        def _():
            part_wait(1, part_z, nz)
            part_y[g] = jnp.sum(part_z[...], axis=0)
            send_parts(2, part_y, g, peers_y)
            send_own(*own_copies, range(2, 6))

        block = h[s]
        as_left(block, left.at[s])
        as_right(block, tmp_b)
        out[s] = mul(left[0], tmp_b[...])

    @pl.when(relays)
    def _():
        for c in range(CHUNKS):
            to_relay(0, c).wait_recv()
            from_relay(c).start()

    send_own(*own_copies, range(2))

    kept_sum[...] = jnp.zeros_like(kept_sum)
    centre[...] = jnp.zeros_like(centre)
    for d in range(6):
        keep_copy(d).wait_recv()

    @pl.loop(0, 6)
    def _(p):
        d = jnp.where(p == 0, near, jnp.where(p == 5, cross, jnp.where(p < 3, p + 3, p - 1)))
        pltpu.make_async_remote_copy(
            src_ref=near_c.at[d],
            dst_ref=near_c.at[d],
            send_sem=c_send.at[0],
            recv_sem=c_recv.at[d],
            device_id=device[0],
            device_id_type=MESH,
        ).wait_recv()
        as_right(near_c[d], couple.at[d])
        both = mul(left[1 + d], couple[d])
        out[0] += both
        kept_sum[...] += near_keep[d, 0:1] * both

    squares[0] = keep[0, 0:1] * out[0]
    send_own(*squares_copies)

    part_wait(2, part_y, ny)
    norm = jnp.sum(jnp.sum(part_y[...], axis=0), keepdims=True)
    norm = jnp.broadcast_to(norm, (8, width)) / count
    factor = 1.0 / jnp.sqrt(norm)
    scale_sq[...] = 1.0 / norm
    for s in range(7):
        scale[s] = factor * keep[s]

    @pl.loop(0, 6)
    def _(p):
        d = jnp.where(p == 0, near, jnp.where(p == 3, cross, jnp.where(p < 3, p + 3, p - 2)))

        @pl.when(p == 2)
        def _():
            as_left(scale_sq[0:1] * kept_sum[...], tmp_a)
            centre[...] += mul(tmp_a[...], first[...])
            as_right(scale_sq[0:1] * squares[0], tmp_b)
            centre[...] += mul(left[0], tmp_b[...])

        @pl.when(p < CHUNKS)
        def _():
            pass_chunk(p, near_o, o_send, o_recv)

        @pl.when(p > 3)
        def _():
            pass_chunk(p - 4, squares, s_send, s_recv)

        @pl.when(p != 3)
        def _():
            for c in range(CHUNKS):
                arrival(d, c, near_o, o_send, o_recv).wait_recv()

        as_right(near_o[1 + d], tmp_b)
        with_own = mul(left[1 + d], tmp_b[...])
        as_right((scale_sq[0:1] * keep[1 + d, 0:1]) * (out[1 + d] + with_own), tmp_b)
        as_left((scale_sq[0:1] * near_keep[d, 0:1]) * with_own, tmp_a)
        out[1 + d] = scale[1 + d, 0:1] * (
            1.5 * h[1 + d] - 0.5 * mul(left[0], tmp_b[...])
        )
        centre[...] += mul(tmp_a[...], couple[d])

    @pl.loop(0, 4)
    def _(p):
        d = jnp.where(p == 0, near, jnp.where(p == 3, cross, p + 3))

        @pl.when(p == 1)
        def _():
            pass_chunk(CHUNKS - 1, squares, s_send, s_recv)
            out[0] = scale[0, 0:1] * (1.5 * h[0] - 0.5 * centre[...])

        @pl.when(p != 3)
        def _():
            for c in range(CHUNKS):
                arrival(d, c, squares, s_send, s_recv).wait_recv()

        as_right(scale_sq[0:1] * squares[1 + d], tmp_b)
        out[1 + d] -= (0.5 * scale[1 + d, 0:1]) * mul(left[1 + d], tmp_b[...])

    @pl.loop(0, 2 * CHUNKS)
    def _(q):
        d, c = 2 + lax.rem(q, 2), q // 2
        arrival(d, c, squares, s_send, s_recv).wait_recv()
        as_right_chunk(scale_sq[0:1] * squares[1 + d, chunk(c)], tmp_b, 0)
        columns = pl.ds(pl.multiple_of(3 * c * rows, 3 * rows), 3 * rows)
        out[1 + d] -= (0.5 * scale[1 + d, 0:1]) * mul(
            left[1 + d, :, columns], tmp_b[0 : 3 * rows]
        )

    @pl.when(relays)
    def _():
        pltpu.make_async_remote_copy(
            src_ref=relay,
            dst_ref=relay,
            send_sem=relay_send.at[0],
            recv_sem=relay_recv.at[0],
            device_id=relay_to,
            device_id_type=MESH,
        ).wait_send()

    for d in range(6):
        keep_copy(d).wait_send()
        couple_copy(d).wait_send()
        for c in range(CHUNKS):
            own_copy(d, c, *own_copies).wait_send()
            own_copy(d, c, *squares_copies).wait_send()


def write_out(result, out_hbm, sem):
    copies = [
        pltpu.make_async_copy(result.at[s], out_hbm.at[s], sem.at[s]) for s in range(7)
    ]
    for copy in copies:
        copy.start()
    for copy in copies:
        copy.wait()


def body(hamiltonian, keep_mask):
    blocks = hamiltonian[0, 0, 0]
    width = blocks.shape[-1]
    sizes = tuple(lax.axis_size(n) for n in ("gx", "gy", "gz"))
    keep = keep_mask[0, 0, 0]
    count = float(sizes[0] * sizes[1] * sizes[2] * width)
    square = (width, width)
    dma = pltpu.SemaphoreType.DMA
    vmem = pltpu.VMEM
    result = pl.pallas_call(
        functools.partial(kernel, sizes, count),
        out_shape=vmem((7, *square), F32),
        in_specs=[
            pl.BlockSpec(memory_space=pltpu.HBM),
            pl.BlockSpec(memory_space=pltpu.SMEM),
        ],
        out_specs=pl.BlockSpec(memory_space=vmem),
        scratch_shapes=[
            vmem((7, *square), F32),
            vmem((6, *square), F32),
            vmem((7, *square), F32),
            vmem((7, *square), F32),
            vmem((7, 8, width), F32),
            vmem((6, 8, width), F32),
            vmem(square, F32),
            vmem((7, width, 3 * width), BF16),
            vmem((6, 3 * width, width), BF16),
            vmem((3 * width, width), BF16),
            vmem((width, 3 * width), BF16),
            vmem((3 * width, width), BF16),
            vmem(square, F32),
            vmem(square, F32),
            vmem((8, width), F32),
            vmem((7, 8, width), F32),
            vmem((sizes[0], 8, 128), F32),
            vmem((sizes[1], 8, 128), F32),
            vmem((sizes[2], 8, 128), F32),
            dma((7,)),
            dma((6,)),
            dma((6,)),
            dma((3,)),
            dma((3,)),
            dma((6,)),
            dma((6,)),
            dma((1,)),
            dma((CHUNKS,)),
            dma((6, CHUNKS)),
            dma((6, CHUNKS)),
            dma((6, CHUNKS)),
            dma((6, CHUNKS)),
        ],
        compiler_params=pltpu.CompilerParams(
            collective_id=0, has_side_effects=True, vmem_limit_bytes=56 << 20
        ),
        name="sign_step",
    )(blocks, keep)
    result = pl.pallas_call(
        write_out,
        out_shape=jax.ShapeDtypeStruct((7, *square), F32),
        in_specs=[pl.BlockSpec(memory_space=vmem)],
        out_specs=pl.BlockSpec(memory_space=pltpu.HBM),
        scratch_shapes=[dma((7,))],
        compiler_params=pltpu.CompilerParams(vmem_limit_bytes=6 << 20),
        name="write_out",
    )(result)
    return result[None, None, None]


def solution(mesh):
    placed = (P("gx", "gy", "gz", None, None, None), P("gx", "gy", "gz", None))
    return jax.shard_map(
        body,
        mesh=mesh,
        in_specs=placed,
        out_specs=P("gx", "gy", "gz", None, None, None),
        check_vma=False,
    )
```

```python
import functools

import jax
import jax.numpy as jnp
from jax import lax
from jax.experimental import pallas as pl
from jax.experimental.pallas import tpu as pltpu
from jax.sharding import PartitionSpec as P

MESH = pl.DeviceIdType.MESH
F32 = jnp.float32
BF16 = jnp.bfloat16
CHUNKS = 3
PIECES = 6


def kernel(
    sizes,
    count,
    h_hbm,
    keep_in,
    out,
    h,
    near_c,
    near_o,
    squares,
    keep,
    near_keep,
    relay,
    left,
    couple,
    first,
    tmp_a,
    tmp_b,
    kept_sum,
    centre,
    scale_sq,
    scale,
    part_x,
    part_y,
    part_z,
    load_sem,
    keep_send,
    keep_recv,
    part_send,
    part_recv,
    c_send,
    c_recv,
    relay_send,
    relay_recv,
    o_send,
    o_recv,
    s_send,
    s_recv,
):
    nx, ny, nz = sizes
    width = h.shape[-1]
    rows = width // CHUNKS
    a, g, z = (lax.axis_index(n) for n in ("gx", "gy", "gz"))
    half = ny // 2
    at_top = lax.rem(g, half) == half - 1
    at_bottom = lax.rem(g, half) == 0
    edge = at_top | at_bottom
    up_x, down_x = lax.rem(a + 1, nx), lax.rem(a + nx - 1, nx)
    up_y, down_y = lax.rem(g + 1, ny), lax.rem(g + ny - 1, ny)
    up_z, down_z = lax.rem(z + 1, nz), lax.rem(z + nz - 1, nz)
    device = [
        (up_x, g, z),
        (down_x, g, z),
        (a, up_y, z),
        (a, down_y, z),
        (a, g, up_z),
        (a, g, down_z),
    ]
    across = nx - 1 - a
    cross = 1 - lax.rem(a, 2)
    near = 1 - cross
    passed_on = {2: (across, up_y, z), 3: (across, down_y, z)}
    wraps = {2: at_top, 3: at_bottom}
    even = lax.rem(a, 2) == 0
    inner = jnp.logical_not(edge)
    above = lax.rem(g, half) == half - 2
    relay_to = (a, lax.rem(g + jnp.where(above, 2, ny - 2), ny), z)

    def chunk(c):
        return pl.ds(pl.multiple_of(c * rows, rows), rows)

    def piece(c):
        size = width // PIECES
        return pl.ds(pl.multiple_of(c * size, size), size)

    barrier = pltpu.get_barrier_semaphore()
    peers_x = [(lax.rem(a + k, nx), g, z) for k in range(1, nx)]
    peers_y = [(a, lax.rem(g + k, ny), z) for k in range(1, ny)]
    peers_z = [(a, g, lax.rem(z + k, nz)) for k in range(1, nz)]
    for peer in peers_x + peers_y + peers_z:
        pl.semaphore_signal(barrier, inc=1, device_id=peer, device_id_type=MESH)
    for d in (2, 3):

        @pl.when(wraps[d])
        def _():
            pl.semaphore_signal(
                barrier, inc=1, device_id=passed_on[d], device_id_type=MESH
            )

    loads = [
        pltpu.make_async_copy(h_hbm.at[s], h.at[s], load_sem.at[s]) for s in range(7)
    ]
    for load in loads:
        load.start()
    for s in range(7):
        keep[s] = jnp.full((8, width), keep_in[s].astype(F32))
    total = jnp.zeros((8, 128), F32)
    for s in range(7):
        loads[s].wait()
        block = h[s]
        squared = jnp.sum((block * block).reshape(width // 8, 8, width), axis=0)
        for j in range(width // 128):
            total = total + squared[:, j * 128 : (j + 1) * 128]
    part_x[a] = total
    pl.semaphore_wait(barrier, nx + ny + nz - 3 + jnp.where(edge, 1, 0))

    def part_copies(stage, buffer, me, peers):
        return [
            pltpu.make_async_remote_copy(
                src_ref=buffer.at[me],
                dst_ref=buffer.at[me],
                send_sem=part_send.at[stage],
                recv_sem=part_recv.at[stage],
                device_id=peer,
                device_id_type=MESH,
            )
            for peer in peers
        ]

    def part_wait(stage, buffer, n):
        copy = pltpu.make_async_remote_copy(
            src_ref=buffer.at[pl.ds(0, n - 1)],
            dst_ref=buffer.at[pl.ds(0, n - 1)],
            send_sem=part_send.at[stage],
            recv_sem=part_recv.at[stage],
            device_id=device[0],
            device_id_type=MESH,
        )
        copy.wait_send()
        copy.wait_recv()

    def keep_copy(d):
        return pltpu.make_async_remote_copy(
            src_ref=keep.at[1 + d],
            dst_ref=near_keep.at[d ^ 1],
            send_sem=keep_send.at[d],
            recv_sem=keep_recv.at[d ^ 1],
            device_id=device[d],
            device_id_type=MESH,
        )

    def couple_copy(d):
        return pltpu.make_async_remote_copy(
            src_ref=h_hbm.at[1 + d],
            dst_ref=near_c.at[d ^ 1],
            send_sem=c_send.at[d],
            recv_sem=c_recv.at[d ^ 1],
            device_id=device[d],
            device_id_type=MESH,
        )

    def to_relay(d, c):
        return pltpu.make_async_remote_copy(
            src_ref=h_hbm.at[1 + d, chunk(c)],
            dst_ref=relay.at[chunk(c)],
            send_sem=c_send.at[d],
            recv_sem=relay_recv.at[c],
            device_id=device[d ^ 1],
            device_id_type=MESH,
        )

    def to_wrap(d, c):
        return pltpu.make_async_remote_copy(
            src_ref=h_hbm.at[1 + d, chunk(c)],
            dst_ref=near_c.at[d ^ 1, chunk(c)],
            send_sem=c_send.at[d],
            recv_sem=c_recv.at[d ^ 1],
            device_id=device[d],
            device_id_type=MESH,
        )

    def from_relay(c):
        return pltpu.make_async_remote_copy(
            src_ref=relay.at[chunk(c)],
            dst_ref=near_c.at[jnp.where(above, 3, 2), chunk(c)],
            send_sem=relay_send.at[min(c, 1)],
            recv_sem=c_recv.at[jnp.where(above, 3, 2)],
            device_id=relay_to,
            device_id_type=MESH,
        )

    def own_copy(d, c, source, target, send, recv):
        return pltpu.make_async_remote_copy(
            src_ref=source.at[0, piece(c)],
            dst_ref=target.at[1 + (d ^ 1), piece(c)],
            send_sem=send.at[d, c],
            recv_sem=recv.at[d ^ 1, c],
            device_id=device[d],
            device_id_type=MESH,
        )

    def pass_copy(d, c, target, send, recv):
        return pltpu.make_async_remote_copy(
            src_ref=target.at[1 + cross, piece(c)],
            dst_ref=target.at[1 + (d ^ 1), piece(c)],
            send_sem=send.at[d, c],
            recv_sem=recv.at[d ^ 1, c],
            device_id=passed_on[d],
            device_id_type=MESH,
        )

    def arrival(d, c, target, send, recv):
        return pltpu.make_async_remote_copy(
            src_ref=target.at[1 + d, piece(c)],
            dst_ref=target.at[1 + d, piece(c)],
            send_sem=send.at[0, c],
            recv_sem=recv.at[d, c],
            device_id=device[0],
            device_id_type=MESH,
        )

    def send_own(source, target, send, recv, directions=range(6)):
        for c in range(PIECES):
            for d in directions:
                copy = own_copy(d, c, source, target, send, recv)
                if d in wraps:
                    pl.when(jnp.logical_not(wraps[d]))(copy.start)
                else:
                    copy.start()

    def pass_piece(c, target, send, recv):
        arrival(cross, c, target, send, recv).wait_recv()
        for d in (2, 3):
            pl.when(wraps[d])(pass_copy(d, c, target, send, recv).start)

    squares_copies = (squares, squares, s_send, s_recv)
    own_copies = (h_hbm, near_o, o_send, o_recv)

    def parts(x):
        high = x.astype(BF16)
        return high, (x - high.astype(F32)).astype(BF16)

    def as_left(x, ref):
        for c in range(CHUNKS):
            high, low = parts(x[:, c * rows : (c + 1) * rows])
            base = 3 * c * rows
            ref[:, base : base + rows] = high
            ref[:, base + rows : base + 2 * rows] = high
            ref[:, base + 2 * rows : base + 3 * rows] = low

    def as_right_chunk(x, ref, base):
        high, low = parts(x)
        ref[pl.ds(base, rows)] = high
        ref[pl.ds(base + rows, rows)] = low
        ref[pl.ds(base + 2 * rows, rows)] = high

    def as_right(x, ref):
        for c in range(CHUNKS):
            as_right_chunk(x[c * rows : (c + 1) * rows], ref, 3 * c * rows)

    def mul(x, y):
        return jnp.dot(x, y, preferred_element_type=F32)

    as_left(h[0], left.at[0])
    as_right(h[0], first)

    def send_parts(stage, buffer, me, peers):
        for copy in part_copies(stage, buffer, me, peers):
            copy.start()

    def send_couples(*directions):
        for d in directions:
            keep_copy(d).start()
        for d in directions:
            if d in wraps:

                for c in range(CHUNKS):
                    if c == 0:
                        pl.when(wraps[d])(to_relay(d, c).start)
                    else:
                        pl.when(wraps[d] & even)(to_relay(d, c).start)
                        pl.when(wraps[d] & jnp.logical_not(even))(to_wrap(d, c).start)
        for d in directions:
            if d in wraps:
                pl.when(jnp.logical_not(wraps[d]))(couple_copy(d).start)
            else:
                couple_copy(d).start()

    send_parts(0, part_x, a, peers_x)
    send_couples(0, 1, 2, 3)

    @pl.loop(0, 7)
    def _(s):
        @pl.when(s == 1)
        def _():
            part_wait(0, part_x, nx)
            part_z[z] = jnp.sum(part_x[...], axis=0)
            send_parts(1, part_z, z, peers_z)
            send_couples(4, 5)

        @pl.when(s == 4)
        def _():
            part_wait(1, part_z, nz)
            part_y[g] = jnp.sum(part_z[...], axis=0)
            send_parts(2, part_y, g, peers_y)
            send_own(*own_copies, range(2, 6))

        block = h[s]
        as_left(block, left.at[s])
        as_right(block, tmp_b)
        out[s] = mul(left[0], tmp_b[...])

    def relay_chunks(*chunks):
        for c in chunks:
            to_relay(0, c).wait_recv()
            from_relay(c).start()

    pl.when(inner)(functools.partial(relay_chunks, 0))
    pl.when(inner & even)(functools.partial(relay_chunks, *range(1, CHUNKS)))

    @pl.when(edge)
    def _():
        send_own(*own_copies, range(2))

    kept_sum[...] = jnp.zeros_like(kept_sum)
    centre[...] = jnp.zeros_like(centre)
    for d in range(6):
        keep_copy(d).wait_recv()

    @pl.loop(0, 6)
    def _(p):
        d = jnp.where(p == 0, near, jnp.where(p == 3, cross, jnp.where(p < 3, p + 3, p - 2)))

        @pl.when((p == 3) & jnp.logical_not(edge))
        def _():
            send_own(*own_copies, range(2))

        @pl.when(p == 5)
        def _():
            pass_piece(0, near_o, o_send, o_recv)
            pass_piece(1, near_o, o_send, o_recv)

        pltpu.make_async_remote_copy(
            src_ref=near_c.at[d],
            dst_ref=near_c.at[d],
            send_sem=c_send.at[0],
            recv_sem=c_recv.at[d],
            device_id=device[0],
            device_id_type=MESH,
        ).wait_recv()
        as_right(near_c[d], couple.at[d])
        both = mul(left[1 + d], couple[d])
        out[0] += both
        kept_sum[...] += near_keep[d, 0:1] * both

    squares[0] = keep[0, 0:1] * out[0]
    send_own(*squares_copies)

    part_wait(2, part_y, ny)
    norm = jnp.sum(jnp.sum(part_y[...], axis=0), keepdims=True)
    norm = jnp.broadcast_to(norm, (8, width)) / count
    factor = 1.0 / jnp.sqrt(norm)
    scale_sq[...] = 1.0 / norm
    for s in range(7):
        scale[s] = factor * keep[s]

    @pl.loop(0, 6)
    def _(p):
        d = jnp.where(p == 0, near, jnp.where(p == 3, cross, jnp.where(p < 3, p + 3, p - 2)))

        @pl.when(p < 2)
        def _():
            pass_piece(2 * p + 2, near_o, o_send, o_recv)
            pass_piece(2 * p + 3, near_o, o_send, o_recv)

        @pl.when(p == 1)
        def _():
            as_left(scale_sq[0:1] * kept_sum[...], tmp_a)
            centre[...] += mul(tmp_a[...], first[...])
            as_right(scale_sq[0:1] * squares[0], tmp_b)
            centre[...] += mul(left[0], tmp_b[...])

        @pl.when(p == 3)
        def _():
            pass_piece(0, squares, s_send, s_recv)

        @pl.when(p >= 3)
        def _():
            pass_piece(p - 2, squares, s_send, s_recv)

        @pl.when(p != 3)
        def _():
            for c in range(PIECES):
                arrival(d, c, near_o, o_send, o_recv).wait_recv()

        as_right(near_o[1 + d], tmp_b)
        with_own = mul(left[1 + d], tmp_b[...])
        as_right((scale_sq[0:1] * keep[1 + d, 0:1]) * (out[1 + d] + with_own), tmp_b)
        as_left((scale_sq[0:1] * near_keep[d, 0:1]) * with_own, tmp_a)
        out[1 + d] = scale[1 + d, 0:1] * (
            1.5 * h[1 + d] - 0.5 * mul(left[0], tmp_b[...])
        )
        centre[...] += mul(tmp_a[...], couple[d])

    @pl.loop(0, 4)
    def _(p):
        d = jnp.where(p == 0, near, jnp.where(p == 3, cross, p + 3))

        @pl.when(p < 2)
        def _():
            pass_piece(4 + p, squares, s_send, s_recv)

        @pl.when(p == 1)
        def _():
            out[0] = scale[0, 0:1] * (1.5 * h[0] - 0.5 * centre[...])

        @pl.when(p != 3)
        def _():
            for c in range(PIECES):
                arrival(d, c, squares, s_send, s_recv).wait_recv()

        as_right(scale_sq[0:1] * squares[1 + d], tmp_b)
        out[1 + d] -= (0.5 * scale[1 + d, 0:1]) * mul(left[1 + d], tmp_b[...])

    @pl.loop(0, 2 * CHUNKS)
    def _(q):
        d, c = 2 + lax.rem(q, 2), q // 2
        for k in range(PIECES // CHUNKS):
            arrival(
                d, PIECES // CHUNKS * c + k, squares, s_send, s_recv
            ).wait_recv()
        as_right_chunk(scale_sq[0:1] * squares[1 + d, chunk(c)], tmp_b, 0)
        columns = pl.ds(pl.multiple_of(3 * c * rows, 3 * rows), 3 * rows)
        out[1 + d] -= (0.5 * scale[1 + d, 0:1]) * mul(
            left[1 + d, :, columns], tmp_b[0 : 3 * rows]
        )

    def relay_left(first, n):
        part = relay.at[pl.ds(first * rows, n * rows)]
        pltpu.make_async_remote_copy(
            src_ref=part,
            dst_ref=part,
            send_sem=relay_send.at[first],
            recv_sem=relay_recv.at[first],
            device_id=relay_to,
            device_id_type=MESH,
        ).wait_send()

    pl.when(inner)(functools.partial(relay_left, 0, 1))
    pl.when(inner & even)(functools.partial(relay_left, 1, CHUNKS - 1))

    for d in range(6):
        keep_copy(d).wait_send()
        couple_copy(d).wait_send()
        for c in range(PIECES):
            own_copy(d, c, *own_copies).wait_send()
            own_copy(d, c, *squares_copies).wait_send()


def write_out(result, out_hbm, sem):
    copies = [
        pltpu.make_async_copy(result.at[s], out_hbm.at[s], sem.at[s]) for s in range(7)
    ]
    for copy in copies:
        copy.start()
    for copy in copies:
        copy.wait()


def body(hamiltonian, keep_mask):
    blocks = hamiltonian[0, 0, 0]
    width = blocks.shape[-1]
    sizes = tuple(lax.axis_size(n) for n in ("gx", "gy", "gz"))
    keep = keep_mask[0, 0, 0]
    count = float(sizes[0] * sizes[1] * sizes[2] * width)
    square = (width, width)
    dma = pltpu.SemaphoreType.DMA
    vmem = pltpu.VMEM
    result = pl.pallas_call(
        functools.partial(kernel, sizes, count),
        out_shape=vmem((7, *square), F32),
        in_specs=[
            pl.BlockSpec(memory_space=pltpu.HBM),
            pl.BlockSpec(memory_space=pltpu.SMEM),
        ],
        out_specs=pl.BlockSpec(memory_space=vmem),
        scratch_shapes=[
            vmem((7, *square), F32),
            vmem((6, *square), F32),
            vmem((7, *square), F32),
            vmem((7, *square), F32),
            vmem((7, 8, width), F32),
            vmem((6, 8, width), F32),
            vmem(square, F32),
            vmem((7, width, 3 * width), BF16),
            vmem((6, 3 * width, width), BF16),
            vmem((3 * width, width), BF16),
            vmem((width, 3 * width), BF16),
            vmem((3 * width, width), BF16),
            vmem(square, F32),
            vmem(square, F32),
            vmem((8, width), F32),
            vmem((7, 8, width), F32),
            vmem((sizes[0], 8, 128), F32),
            vmem((sizes[1], 8, 128), F32),
            vmem((sizes[2], 8, 128), F32),
            dma((7,)),
            dma((6,)),
            dma((6,)),
            dma((3,)),
            dma((3,)),
            dma((6,)),
            dma((6,)),
            dma((2,)),
            dma((CHUNKS,)),
            dma((6, PIECES)),
            dma((6, PIECES)),
            dma((6, PIECES)),
            dma((6, PIECES)),
        ],
        compiler_params=pltpu.CompilerParams(
            collective_id=0, has_side_effects=True, vmem_limit_bytes=56 << 20
        ),
        name="sign_step",
    )(blocks, keep)
    result = pl.pallas_call(
        write_out,
        out_shape=jax.ShapeDtypeStruct((7, *square), F32),
        in_specs=[pl.BlockSpec(memory_space=vmem)],
        out_specs=pl.BlockSpec(memory_space=pltpu.HBM),
        scratch_shapes=[dma((7,))],
        compiler_params=pltpu.CompilerParams(vmem_limit_bytes=6 << 20),
        name="write_out",
    )(result)
    return result[None, None, None]


def solution(mesh):
    placed = (P("gx", "gy", "gz", None, None, None), P("gx", "gy", "gz", None))
    return jax.shard_map(
        body,
        mesh=mesh,
        in_specs=placed,
        out_specs=P("gx", "gy", "gz", None, None, None),
        check_vma=False,
    )
```

```python
import functools

import jax
import jax.numpy as jnp
from jax import lax
from jax.experimental import pallas as pl
from jax.experimental.pallas import tpu as pltpu
from jax.sharding import PartitionSpec as P

MESH = pl.DeviceIdType.MESH
F32 = jnp.float32
BF16 = jnp.bfloat16
CHUNKS = 3
PIECES = 6


def kernel(
    sizes,
    count,
    h_hbm,
    keep_in,
    out,
    h,
    near_c,
    near_o,
    squares,
    keep,
    near_keep,
    relay,
    left,
    couple,
    first,
    tmp_a,
    tmp_b,
    kept_sum,
    centre,
    scale_sq,
    scale,
    part_x,
    part_y,
    part_z,
    load_sem,
    keep_send,
    keep_recv,
    part_send,
    part_recv,
    c_send,
    c_recv,
    relay_send,
    relay_recv,
    o_send,
    o_recv,
    s_send,
    s_recv,
):
    nx, ny, nz = sizes
    width = h.shape[-1]
    rows = width // CHUNKS
    a, g, z = (lax.axis_index(n) for n in ("gx", "gy", "gz"))
    half = ny // 2
    at_top = lax.rem(g, half) == half - 1
    at_bottom = lax.rem(g, half) == 0
    edge = at_top | at_bottom
    up_x, down_x = lax.rem(a + 1, nx), lax.rem(a + nx - 1, nx)
    up_y, down_y = lax.rem(g + 1, ny), lax.rem(g + ny - 1, ny)
    up_z, down_z = lax.rem(z + 1, nz), lax.rem(z + nz - 1, nz)
    device = [
        (up_x, g, z),
        (down_x, g, z),
        (a, up_y, z),
        (a, down_y, z),
        (a, g, up_z),
        (a, g, down_z),
    ]
    across = nx - 1 - a
    cross = 1 - lax.rem(a, 2)
    near = 1 - cross
    passed_on = {2: (across, up_y, z), 3: (across, down_y, z)}
    wraps = {2: at_top, 3: at_bottom}
    wrapped = jnp.where(at_top, 2, 3)
    late = [
        jnp.where(edge, cross, 2),
        jnp.where(edge, 5 - wrapped, 3),
        jnp.where(edge, wrapped, cross),
    ]
    even = lax.rem(a, 2) == 0
    inner = jnp.logical_not(edge)
    above = lax.rem(g, half) == half - 2
    relay_to = (a, lax.rem(g + jnp.where(above, 2, ny - 2), ny), z)

    def chunk(c):
        return pl.ds(pl.multiple_of(c * rows, rows), rows)

    def piece(c):
        size = width // PIECES
        return pl.ds(pl.multiple_of(c * size, size), size)

    barrier = pltpu.get_barrier_semaphore()
    peers_x = [(lax.rem(a + k, nx), g, z) for k in range(1, nx)]
    peers_y = [(a, lax.rem(g + k, ny), z) for k in range(1, ny)]
    peers_z = [(a, g, lax.rem(z + k, nz)) for k in range(1, nz)]
    for peer in peers_x + peers_y + peers_z:
        pl.semaphore_signal(barrier, inc=1, device_id=peer, device_id_type=MESH)
    for d in (2, 3):

        @pl.when(wraps[d])
        def _():
            pl.semaphore_signal(
                barrier, inc=1, device_id=passed_on[d], device_id_type=MESH
            )

    loads = [
        pltpu.make_async_copy(h_hbm.at[s], h.at[s], load_sem.at[s]) for s in range(7)
    ]
    for load in loads:
        load.start()
    for s in range(7):
        keep[s] = jnp.full((8, width), keep_in[s].astype(F32))
    total = jnp.zeros((8, 128), F32)
    for s in range(7):
        loads[s].wait()
        block = h[s]
        squared = jnp.sum((block * block).reshape(width // 8, 8, width), axis=0)
        for j in range(width // 128):
            total = total + squared[:, j * 128 : (j + 1) * 128]
    part_x[a] = total
    pl.semaphore_wait(barrier, nx + ny + nz - 3 + jnp.where(edge, 1, 0))

    def part_copies(stage, buffer, me, peers):
        return [
            pltpu.make_async_remote_copy(
                src_ref=buffer.at[me],
                dst_ref=buffer.at[me],
                send_sem=part_send.at[stage],
                recv_sem=part_recv.at[stage],
                device_id=peer,
                device_id_type=MESH,
            )
            for peer in peers
        ]

    def part_wait(stage, buffer, n):
        copy = pltpu.make_async_remote_copy(
            src_ref=buffer.at[pl.ds(0, n - 1)],
            dst_ref=buffer.at[pl.ds(0, n - 1)],
            send_sem=part_send.at[stage],
            recv_sem=part_recv.at[stage],
            device_id=device[0],
            device_id_type=MESH,
        )
        copy.wait_send()
        copy.wait_recv()

    def keep_copy(d):
        return pltpu.make_async_remote_copy(
            src_ref=keep.at[1 + d],
            dst_ref=near_keep.at[d ^ 1],
            send_sem=keep_send.at[d],
            recv_sem=keep_recv.at[d ^ 1],
            device_id=device[d],
            device_id_type=MESH,
        )

    def couple_copy(d):
        return pltpu.make_async_remote_copy(
            src_ref=h_hbm.at[1 + d],
            dst_ref=near_c.at[d ^ 1],
            send_sem=c_send.at[d],
            recv_sem=c_recv.at[d ^ 1],
            device_id=device[d],
            device_id_type=MESH,
        )

    def to_relay(d, c):
        return pltpu.make_async_remote_copy(
            src_ref=h_hbm.at[1 + d, chunk(c)],
            dst_ref=relay.at[chunk(c)],
            send_sem=c_send.at[d],
            recv_sem=relay_recv.at[c],
            device_id=device[d ^ 1],
            device_id_type=MESH,
        )

    def to_wrap(d, c):
        return pltpu.make_async_remote_copy(
            src_ref=h_hbm.at[1 + d, chunk(c)],
            dst_ref=near_c.at[d ^ 1, chunk(c)],
            send_sem=c_send.at[d],
            recv_sem=c_recv.at[d ^ 1],
            device_id=device[d],
            device_id_type=MESH,
        )

    def from_relay(c):
        return pltpu.make_async_remote_copy(
            src_ref=relay.at[chunk(c)],
            dst_ref=near_c.at[jnp.where(above, 3, 2), chunk(c)],
            send_sem=relay_send.at[min(c, 1)],
            recv_sem=c_recv.at[jnp.where(above, 3, 2)],
            device_id=relay_to,
            device_id_type=MESH,
        )

    def own_copy(d, c, source, target, send, recv):
        return pltpu.make_async_remote_copy(
            src_ref=source.at[0, piece(c)],
            dst_ref=target.at[1 + (d ^ 1), piece(c)],
            send_sem=send.at[d, c],
            recv_sem=recv.at[d ^ 1, c],
            device_id=device[d],
            device_id_type=MESH,
        )

    def pass_copy(d, c, target, send, recv):
        return pltpu.make_async_remote_copy(
            src_ref=target.at[1 + cross, piece(c)],
            dst_ref=target.at[1 + (d ^ 1), piece(c)],
            send_sem=send.at[d, c],
            recv_sem=recv.at[d ^ 1, c],
            device_id=passed_on[d],
            device_id_type=MESH,
        )

    def arrival(d, c, target, send, recv):
        return pltpu.make_async_remote_copy(
            src_ref=target.at[1 + d, piece(c)],
            dst_ref=target.at[1 + d, piece(c)],
            send_sem=send.at[0, c],
            recv_sem=recv.at[d, c],
            device_id=device[0],
            device_id_type=MESH,
        )

    def send_own(source, target, send, recv, directions=range(6)):
        for c in range(PIECES):
            for d in directions:
                copy = own_copy(d, c, source, target, send, recv)
                if d in wraps:
                    pl.when(jnp.logical_not(wraps[d]))(copy.start)
                else:
                    copy.start()

    def awaits(d):
        return jnp.logical_not(edge & (d == cross))

    def pass_piece(c, target, send, recv):
        arrival(cross, c, target, send, recv).wait_recv()
        for d in (2, 3):
            pl.when(wraps[d])(pass_copy(d, c, target, send, recv).start)

    squares_copies = (squares, squares, s_send, s_recv)
    own_copies = (h_hbm, near_o, o_send, o_recv)

    def parts(x):
        high = x.astype(BF16)
        return high, (x - high.astype(F32)).astype(BF16)

    def as_left(x, ref):
        for c in range(CHUNKS):
            high, low = parts(x[:, c * rows : (c + 1) * rows])
            base = 3 * c * rows
            ref[:, base : base + rows] = high
            ref[:, base + rows : base + 2 * rows] = high
            ref[:, base + 2 * rows : base + 3 * rows] = low

    def as_right_chunk(x, ref, base):
        high, low = parts(x)
        ref[pl.ds(base, rows)] = high
        ref[pl.ds(base + rows, rows)] = low
        ref[pl.ds(base + 2 * rows, rows)] = high

    def as_right(x, ref):
        for c in range(CHUNKS):
            as_right_chunk(x[c * rows : (c + 1) * rows], ref, 3 * c * rows)

    def mul(x, y):
        return jnp.dot(x, y, preferred_element_type=F32)

    as_left(h[0], left.at[0])
    as_right(h[0], first)

    def send_parts(stage, buffer, me, peers):
        for copy in part_copies(stage, buffer, me, peers):
            copy.start()

    def send_couples(*directions):
        for d in directions:
            keep_copy(d).start()
        for d in directions:
            if d in wraps:

                for c in range(CHUNKS):
                    if c == 0:
                        pl.when(wraps[d])(to_relay(d, c).start)
                    else:
                        pl.when(wraps[d] & even)(to_relay(d, c).start)
                        pl.when(wraps[d] & jnp.logical_not(even))(to_wrap(d, c).start)
        for d in directions:
            if d in wraps:
                pl.when(jnp.logical_not(wraps[d]))(couple_copy(d).start)
            else:
                couple_copy(d).start()

    send_parts(0, part_x, a, peers_x)
    send_couples(0, 1, 2, 3)

    @pl.loop(0, 7)
    def _(s):
        @pl.when(s == 1)
        def _():
            part_wait(0, part_x, nx)
            part_z[z] = jnp.sum(part_x[...], axis=0)
            send_parts(1, part_z, z, peers_z)
            send_couples(4, 5)

        @pl.when(s == 4)
        def _():
            part_wait(1, part_z, nz)
            part_y[g] = jnp.sum(part_z[...], axis=0)
            send_parts(2, part_y, g, peers_y)
            send_own(*own_copies, range(2, 6))

        block = h[s]
        as_left(block, left.at[s])
        as_right(block, tmp_b)
        out[s] = mul(left[0], tmp_b[...])

    def relay_chunks(*chunks):
        for c in chunks:
            to_relay(0, c).wait_recv()
            from_relay(c).start()

    pl.when(inner)(functools.partial(relay_chunks, 0))
    pl.when(inner & even)(functools.partial(relay_chunks, *range(1, CHUNKS)))

    @pl.when(edge)
    def _():
        send_own(*own_copies, range(2))

    def direction(p):
        d = jnp.where(p == 0, near, p + 3)
        for k in range(3):
            d = jnp.where(p == 3 + k, late[k], d)
        return d

    kept_sum[...] = jnp.zeros_like(kept_sum)
    centre[...] = jnp.zeros_like(centre)
    for d in range(6):
        keep_copy(d).wait_recv()

    @pl.loop(0, 6)
    def _(p):
        d = direction(p)

        @pl.when((p == 3) & jnp.logical_not(edge))
        def _():
            send_own(*own_copies, range(2))

        @pl.when((p == 5) & edge)
        def _():
            pass_piece(0, near_o, o_send, o_recv)
            pass_piece(1, near_o, o_send, o_recv)

        pltpu.make_async_remote_copy(
            src_ref=near_c.at[d],
            dst_ref=near_c.at[d],
            send_sem=c_send.at[0],
            recv_sem=c_recv.at[d],
            device_id=device[0],
            device_id_type=MESH,
        ).wait_recv()
        as_right(near_c[d], couple.at[d])
        both = mul(left[1 + d], couple[d])
        out[0] += both
        kept_sum[...] += near_keep[d, 0:1] * both

    squares[0] = keep[0, 0:1] * out[0]
    send_own(*squares_copies)

    part_wait(2, part_y, ny)
    norm = jnp.sum(jnp.sum(part_y[...], axis=0), keepdims=True)
    norm = jnp.broadcast_to(norm, (8, width)) / count
    factor = 1.0 / jnp.sqrt(norm)
    scale_sq[...] = 1.0 / norm
    for s in range(7):
        scale[s] = factor * keep[s]

    @pl.loop(0, 6)
    def _(p):
        d = direction(p)

        @pl.when((p < 2) & edge)
        def _():
            pass_piece(2 * p + 2, near_o, o_send, o_recv)
            pass_piece(2 * p + 3, near_o, o_send, o_recv)

        @pl.when(p == 1)
        def _():
            as_left(scale_sq[0:1] * kept_sum[...], tmp_a)
            centre[...] += mul(tmp_a[...], first[...])
            as_right(scale_sq[0:1] * squares[0], tmp_b)
            centre[...] += mul(left[0], tmp_b[...])

        @pl.when((p == 3) & edge)
        def _():
            pass_piece(0, squares, s_send, s_recv)

        @pl.when((p >= 3) & edge)
        def _():
            pass_piece(p - 2, squares, s_send, s_recv)

        @pl.when(awaits(d))
        def _():
            for c in range(PIECES):
                arrival(d, c, near_o, o_send, o_recv).wait_recv()

        as_right(near_o[1 + d], tmp_b)
        with_own = mul(left[1 + d], tmp_b[...])
        as_right((scale_sq[0:1] * keep[1 + d, 0:1]) * (out[1 + d] + with_own), tmp_b)
        as_left((scale_sq[0:1] * near_keep[d, 0:1]) * with_own, tmp_a)
        out[1 + d] = scale[1 + d, 0:1] * (
            1.5 * h[1 + d] - 0.5 * mul(left[0], tmp_b[...])
        )
        centre[...] += mul(tmp_a[...], couple[d])

    @pl.loop(0, 4)
    def _(p):
        d = jnp.where(p == 0, near, p + 3)
        d = jnp.where(p == 3, jnp.where(edge, late[1], late[0]), d)

        @pl.when((p < 2) & edge)
        def _():
            pass_piece(4 + p, squares, s_send, s_recv)

        @pl.when(p == 1)
        def _():
            out[0] = scale[0, 0:1] * (1.5 * h[0] - 0.5 * centre[...])

        for c in range(PIECES):
            arrival(d, c, squares, s_send, s_recv).wait_recv()

        as_right(scale_sq[0:1] * squares[1 + d], tmp_b)
        out[1 + d] -= (0.5 * scale[1 + d, 0:1]) * mul(left[1 + d], tmp_b[...])

    @pl.loop(0, 2 * CHUNKS)
    def _(q):
        earlier = jnp.where(edge, late[0], late[1])
        d, c = jnp.where(lax.rem(q, 2) == 0, earlier, late[2]), q // 2

        @pl.when(awaits(d))
        def _():
            for k in range(PIECES // CHUNKS):
                arrival(
                    d, PIECES // CHUNKS * c + k, squares, s_send, s_recv
                ).wait_recv()

        as_right_chunk(scale_sq[0:1] * squares[1 + d, chunk(c)], tmp_b, 0)
        columns = pl.ds(pl.multiple_of(3 * c * rows, 3 * rows), 3 * rows)
        out[1 + d] -= (0.5 * scale[1 + d, 0:1]) * mul(
            left[1 + d, :, columns], tmp_b[0 : 3 * rows]
        )

    def relay_left(first, n):
        part = relay.at[pl.ds(first * rows, n * rows)]
        pltpu.make_async_remote_copy(
            src_ref=part,
            dst_ref=part,
            send_sem=relay_send.at[first],
            recv_sem=relay_recv.at[first],
            device_id=relay_to,
            device_id_type=MESH,
        ).wait_send()

    pl.when(inner)(functools.partial(relay_left, 0, 1))
    pl.when(inner & even)(functools.partial(relay_left, 1, CHUNKS - 1))

    for d in range(6):
        keep_copy(d).wait_send()
        couple_copy(d).wait_send()
        for c in range(PIECES):
            own_copy(d, c, *own_copies).wait_send()
            own_copy(d, c, *squares_copies).wait_send()


def write_out(result, out_hbm, sem):
    copies = [
        pltpu.make_async_copy(result.at[s], out_hbm.at[s], sem.at[s]) for s in range(7)
    ]
    for copy in copies:
        copy.start()
    for copy in copies:
        copy.wait()


def body(hamiltonian, keep_mask):
    blocks = hamiltonian[0, 0, 0]
    width = blocks.shape[-1]
    sizes = tuple(lax.axis_size(n) for n in ("gx", "gy", "gz"))
    keep = keep_mask[0, 0, 0]
    count = float(sizes[0] * sizes[1] * sizes[2] * width)
    square = (width, width)
    dma = pltpu.SemaphoreType.DMA
    vmem = pltpu.VMEM
    result = pl.pallas_call(
        functools.partial(kernel, sizes, count),
        out_shape=vmem((7, *square), F32),
        in_specs=[
            pl.BlockSpec(memory_space=pltpu.HBM),
            pl.BlockSpec(memory_space=pltpu.SMEM),
        ],
        out_specs=pl.BlockSpec(memory_space=vmem),
        scratch_shapes=[
            vmem((7, *square), F32),
            vmem((6, *square), F32),
            vmem((7, *square), F32),
            vmem((7, *square), F32),
            vmem((7, 8, width), F32),
            vmem((6, 8, width), F32),
            vmem(square, F32),
            vmem((7, width, 3 * width), BF16),
            vmem((6, 3 * width, width), BF16),
            vmem((3 * width, width), BF16),
            vmem((width, 3 * width), BF16),
            vmem((3 * width, width), BF16),
            vmem(square, F32),
            vmem(square, F32),
            vmem((8, width), F32),
            vmem((7, 8, width), F32),
            vmem((sizes[0], 8, 128), F32),
            vmem((sizes[1], 8, 128), F32),
            vmem((sizes[2], 8, 128), F32),
            dma((7,)),
            dma((6,)),
            dma((6,)),
            dma((3,)),
            dma((3,)),
            dma((6,)),
            dma((6,)),
            dma((2,)),
            dma((CHUNKS,)),
            dma((6, PIECES)),
            dma((6, PIECES)),
            dma((6, PIECES)),
            dma((6, PIECES)),
        ],
        compiler_params=pltpu.CompilerParams(
            collective_id=0, has_side_effects=True, vmem_limit_bytes=56 << 20
        ),
        name="sign_step",
    )(blocks, keep)
    result = pl.pallas_call(
        write_out,
        out_shape=jax.ShapeDtypeStruct((7, *square), F32),
        in_specs=[pl.BlockSpec(memory_space=vmem)],
        out_specs=pl.BlockSpec(memory_space=pltpu.HBM),
        scratch_shapes=[dma((7,))],
        compiler_params=pltpu.CompilerParams(vmem_limit_bytes=6 << 20),
        name="write_out",
    )(result)
    return result[None, None, None]


def solution(mesh):
    placed = (P("gx", "gy", "gz", None, None, None), P("gx", "gy", "gz", None))
    return jax.shard_map(
        body,
        mesh=mesh,
        in_specs=placed,
        out_specs=P("gx", "gy", "gz", None, None, None),
        check_vma=False,
    )
```

```python
import functools

import jax
import jax.numpy as jnp
from jax import lax
from jax.experimental import pallas as pl
from jax.experimental.pallas import tpu as pltpu
from jax.sharding import PartitionSpec as P

MESH = pl.DeviceIdType.MESH
F32 = jnp.float32
BF16 = jnp.bfloat16
CHUNKS = 3
PIECES = 6


def kernel(
    sizes,
    count,
    h_hbm,
    keep_in,
    out,
    h,
    near_c,
    near_o,
    squares,
    keep,
    near_keep,
    relay,
    left,
    couple,
    first,
    tmp_a,
    tmp_b,
    kept_sum,
    centre,
    scale_sq,
    scale,
    part_x,
    part_y,
    part_z,
    load_sem,
    keep_send,
    keep_recv,
    part_send,
    part_recv,
    c_send,
    c_recv,
    relay_send,
    relay_recv,
    o_send,
    o_recv,
    s_send,
    s_recv,
):
    nx, ny, nz = sizes
    width = h.shape[-1]
    rows = width // CHUNKS
    a, g, z = (lax.axis_index(n) for n in ("gx", "gy", "gz"))
    half = ny // 2
    at_top = lax.rem(g, half) == half - 1
    at_bottom = lax.rem(g, half) == 0
    edge = at_top | at_bottom
    up_x, down_x = lax.rem(a + 1, nx), lax.rem(a + nx - 1, nx)
    up_y, down_y = lax.rem(g + 1, ny), lax.rem(g + ny - 1, ny)
    up_z, down_z = lax.rem(z + 1, nz), lax.rem(z + nz - 1, nz)
    device = [
        (up_x, g, z),
        (down_x, g, z),
        (a, up_y, z),
        (a, down_y, z),
        (a, g, up_z),
        (a, g, down_z),
    ]
    across = nx - 1 - a
    cross = 1 - lax.rem(a, 2)
    near = 1 - cross
    passed_on = {2: (across, up_y, z), 3: (across, down_y, z)}
    wraps = {2: at_top, 3: at_bottom}
    wrapped = jnp.where(at_top, 2, 3)
    late = [
        jnp.where(edge, cross, 2),
        jnp.where(edge, 5 - wrapped, 3),
        jnp.where(edge, wrapped, cross),
    ]
    even = lax.rem(a, 2) == 0
    inner = jnp.logical_not(edge)
    above = lax.rem(g, half) == half - 2
    relay_to = (a, lax.rem(g + jnp.where(above, 2, ny - 2), ny), z)

    def chunk(c):
        return pl.ds(pl.multiple_of(c * rows, rows), rows)

    def piece(c):
        size = width // PIECES
        return pl.ds(pl.multiple_of(c * size, size), size)

    barrier = pltpu.get_barrier_semaphore()
    peers_x = [(lax.rem(a + k, nx), g, z) for k in range(1, nx)]
    peers_y = [(a, lax.rem(g + k, ny), z) for k in range(1, ny)]
    peers_z = [(a, g, lax.rem(z + k, nz)) for k in range(1, nz)]
    for peer in peers_x + peers_y + peers_z:
        pl.semaphore_signal(barrier, inc=1, device_id=peer, device_id_type=MESH)
    for d in (2, 3):

        @pl.when(wraps[d])
        def _():
            pl.semaphore_signal(
                barrier, inc=1, device_id=passed_on[d], device_id_type=MESH
            )

    loads = [
        pltpu.make_async_copy(h_hbm.at[s], h.at[s], load_sem.at[s]) for s in range(7)
    ]
    for load in loads:
        load.start()
    for s in range(7):
        keep[s] = jnp.full((8, width), keep_in[s].astype(F32))
    total = jnp.zeros((8, 128), F32)
    for s in range(7):
        loads[s].wait()
        block = h[s]
        squared = jnp.sum((block * block).reshape(width // 8, 8, width), axis=0)
        for j in range(width // 128):
            total = total + squared[:, j * 128 : (j + 1) * 128]
    part_x[a] = total
    pl.semaphore_wait(barrier, nx + ny + nz - 3 + jnp.where(edge, 1, 0))

    def part_copies(stage, buffer, me, peers):
        return [
            pltpu.make_async_remote_copy(
                src_ref=buffer.at[me],
                dst_ref=buffer.at[me],
                send_sem=part_send.at[stage],
                recv_sem=part_recv.at[stage],
                device_id=peer,
                device_id_type=MESH,
            )
            for peer in peers
        ]

    def part_wait(stage, buffer, n):
        copy = pltpu.make_async_remote_copy(
            src_ref=buffer.at[pl.ds(0, n - 1)],
            dst_ref=buffer.at[pl.ds(0, n - 1)],
            send_sem=part_send.at[stage],
            recv_sem=part_recv.at[stage],
            device_id=device[0],
            device_id_type=MESH,
        )
        copy.wait_send()
        copy.wait_recv()

    def keep_copy(d):
        return pltpu.make_async_remote_copy(
            src_ref=keep.at[1 + d],
            dst_ref=near_keep.at[d ^ 1],
            send_sem=keep_send.at[d],
            recv_sem=keep_recv.at[d ^ 1],
            device_id=device[d],
            device_id_type=MESH,
        )

    def couple_copy(d):
        return pltpu.make_async_remote_copy(
            src_ref=h_hbm.at[1 + d],
            dst_ref=near_c.at[d ^ 1],
            send_sem=c_send.at[d],
            recv_sem=c_recv.at[d ^ 1],
            device_id=device[d],
            device_id_type=MESH,
        )

    def to_relay(d, c):
        return pltpu.make_async_remote_copy(
            src_ref=h_hbm.at[1 + d, chunk(c)],
            dst_ref=relay.at[chunk(c)],
            send_sem=c_send.at[d],
            recv_sem=relay_recv.at[c],
            device_id=device[d ^ 1],
            device_id_type=MESH,
        )

    def to_wrap(d, c):
        return pltpu.make_async_remote_copy(
            src_ref=h_hbm.at[1 + d, chunk(c)],
            dst_ref=near_c.at[d ^ 1, chunk(c)],
            send_sem=c_send.at[d],
            recv_sem=c_recv.at[d ^ 1],
            device_id=device[d],
            device_id_type=MESH,
        )

    def from_relay(c):
        return pltpu.make_async_remote_copy(
            src_ref=relay.at[chunk(c)],
            dst_ref=near_c.at[jnp.where(above, 3, 2), chunk(c)],
            send_sem=relay_send.at[min(c, 1)],
            recv_sem=c_recv.at[jnp.where(above, 3, 2)],
            device_id=relay_to,
            device_id_type=MESH,
        )

    def own_copy(d, c, source, target, send, recv):
        return pltpu.make_async_remote_copy(
            src_ref=source.at[0, piece(c)],
            dst_ref=target.at[1 + (d ^ 1), piece(c)],
            send_sem=send.at[d],
            recv_sem=recv.at[d ^ 1, c],
            device_id=device[d],
            device_id_type=MESH,
        )

    def pass_copy(d, c, target, send, recv):
        return pltpu.make_async_remote_copy(
            src_ref=target.at[1 + cross, piece(c)],
            dst_ref=target.at[1 + (d ^ 1), piece(c)],
            send_sem=send.at[d],
            recv_sem=recv.at[d ^ 1, c],
            device_id=passed_on[d],
            device_id_type=MESH,
        )

    def arrival(d, c, target, send, recv):
        return pltpu.make_async_remote_copy(
            src_ref=target.at[1 + d, piece(c)],
            dst_ref=target.at[1 + d, piece(c)],
            send_sem=send.at[0],
            recv_sem=recv.at[d, c],
            device_id=device[0],
            device_id_type=MESH,
        )

    def send_own(source, target, send, recv, directions=range(6)):
        for c in range(PIECES):
            for d in directions:
                copy = own_copy(d, c, source, target, send, recv)
                if d in wraps:
                    pl.when(jnp.logical_not(wraps[d]))(copy.start)
                else:
                    copy.start()

    def awaits(d):
        return jnp.logical_not(edge & (d == cross))

    def pass_piece(c, target, send, recv):
        arrival(cross, c, target, send, recv).wait_recv()
        for d in (2, 3):
            pl.when(wraps[d])(pass_copy(d, c, target, send, recv).start)

    squares_copies = (squares, squares, s_send, s_recv)
    own_copies = (h_hbm, near_o, o_send, o_recv)

    def parts(x):
        high = x.astype(BF16)
        return high, (x - high.astype(F32)).astype(BF16)

    def as_left(x, ref):
        for c in range(CHUNKS):
            high, low = parts(x[:, c * rows : (c + 1) * rows])
            base = 3 * c * rows
            ref[:, base : base + rows] = high
            ref[:, base + rows : base + 2 * rows] = high
            ref[:, base + 2 * rows : base + 3 * rows] = low

    def as_right_chunk(x, ref, base):
        high, low = parts(x)
        ref[pl.ds(base, rows)] = high
        ref[pl.ds(base + rows, rows)] = low
        ref[pl.ds(base + 2 * rows, rows)] = high

    def as_right(x, ref):
        for c in range(CHUNKS):
            as_right_chunk(x[c * rows : (c + 1) * rows], ref, 3 * c * rows)

    def mul(x, y):
        return jnp.dot(x, y, preferred_element_type=F32)

    as_left(h[0], left.at[0])
    as_right(h[0], first)

    def send_parts(stage, buffer, me, peers):
        for copy in part_copies(stage, buffer, me, peers):
            copy.start()

    def send_couples(*directions):
        for d in directions:
            keep_copy(d).start()
        for d in directions:
            if d in wraps:

                for c in range(CHUNKS):
                    if c == 0:
                        pl.when(wraps[d])(to_relay(d, c).start)
                    else:
                        pl.when(wraps[d] & even)(to_relay(d, c).start)
                        pl.when(wraps[d] & jnp.logical_not(even))(to_wrap(d, c).start)
        for d in directions:
            if d in wraps:
                pl.when(jnp.logical_not(wraps[d]))(couple_copy(d).start)
            else:
                couple_copy(d).start()

    send_parts(0, part_x, a, peers_x)
    send_couples(0, 1, 2, 3)

    @pl.loop(0, 7)
    def _(s):
        @pl.when(s == 1)
        def _():
            part_wait(0, part_x, nx)
            part_z[z] = jnp.sum(part_x[...], axis=0)
            send_parts(1, part_z, z, peers_z)
            send_couples(4, 5)

        @pl.when(s == 4)
        def _():
            part_wait(1, part_z, nz)
            part_y[g] = jnp.sum(part_z[...], axis=0)
            send_parts(2, part_y, g, peers_y)
            send_own(*own_copies, range(2, 6))

        block = h[s]
        as_left(block, left.at[s])
        as_right(block, tmp_b)
        out[s] = mul(left[0], tmp_b[...])

    def relay_chunks(*chunks):
        for c in chunks:
            to_relay(0, c).wait_recv()
            from_relay(c).start()

    pl.when(inner)(functools.partial(relay_chunks, 0))
    pl.when(inner & even)(functools.partial(relay_chunks, *range(1, CHUNKS)))

    @pl.when(edge)
    def _():
        send_own(*own_copies, range(2))

    def direction(p):
        d = jnp.where(p == 0, near, p + 3)
        for k in range(3):
            d = jnp.where(p == 3 + k, late[k], d)
        return d

    kept_sum[...] = jnp.zeros_like(kept_sum)
    centre[...] = jnp.zeros_like(centre)
    for d in range(6):
        keep_copy(d).wait_recv()

    @pl.loop(0, 6)
    def _(p):
        d = direction(p)

        @pl.when((p == 3) & jnp.logical_not(edge))
        def _():
            send_own(*own_copies, range(2))

        @pl.when((p == 5) & edge)
        def _():
            pass_piece(0, near_o, o_send, o_recv)
            pass_piece(1, near_o, o_send, o_recv)

        pltpu.make_async_remote_copy(
            src_ref=near_c.at[d],
            dst_ref=near_c.at[d],
            send_sem=c_send.at[0],
            recv_sem=c_recv.at[d],
            device_id=device[0],
            device_id_type=MESH,
        ).wait_recv()
        as_right(near_c[d], couple.at[d])
        both = mul(left[1 + d], couple[d])
        out[0] += both
        kept_sum[...] += near_keep[d, 0:1] * both

    squares[0] = keep[0, 0:1] * out[0]
    send_own(*squares_copies)

    part_wait(2, part_y, ny)
    norm = jnp.sum(jnp.sum(part_y[...], axis=0), keepdims=True)
    norm = jnp.broadcast_to(norm, (8, width)) / count
    factor = 1.0 / jnp.sqrt(norm)
    scale_sq[...] = 1.0 / norm
    for s in range(7):
        scale[s] = factor * keep[s]

    @pl.loop(0, 6)
    def _(p):
        d = direction(p)

        @pl.when((p < 2) & edge)
        def _():
            pass_piece(2 * p + 2, near_o, o_send, o_recv)
            pass_piece(2 * p + 3, near_o, o_send, o_recv)

        @pl.when(p == 1)
        def _():
            as_left(scale_sq[0:1] * kept_sum[...], tmp_a)
            centre[...] += mul(tmp_a[...], first[...])
            as_right(scale_sq[0:1] * squares[0], tmp_b)
            centre[...] += mul(left[0], tmp_b[...])

        @pl.when((p == 3) & edge)
        def _():
            pass_piece(0, squares, s_send, s_recv)

        @pl.when((p >= 3) & edge)
        def _():
            pass_piece(p - 2, squares, s_send, s_recv)

        @pl.when(awaits(d))
        def _():
            for c in range(PIECES):
                arrival(d, c, near_o, o_send, o_recv).wait_recv()

        as_right(near_o[1 + d], tmp_b)
        with_own = mul(left[1 + d], tmp_b[...])
        as_right((scale_sq[0:1] * keep[1 + d, 0:1]) * (out[1 + d] + with_own), tmp_b)
        as_left((scale_sq[0:1] * near_keep[d, 0:1]) * with_own, tmp_a)
        out[1 + d] = scale[1 + d, 0:1] * (
            1.5 * h[1 + d] - 0.5 * mul(left[0], tmp_b[...])
        )
        centre[...] += mul(tmp_a[...], couple[d])

    @pl.loop(0, 4)
    def _(p):
        d = jnp.where(p == 0, near, p + 3)
        d = jnp.where(p == 3, jnp.where(edge, late[1], late[0]), d)

        @pl.when((p < 2) & edge)
        def _():
            pass_piece(4 + p, squares, s_send, s_recv)

        @pl.when(p == 1)
        def _():
            out[0] = scale[0, 0:1] * (1.5 * h[0] - 0.5 * centre[...])

        for c in range(PIECES):
            arrival(d, c, squares, s_send, s_recv).wait_recv()

        as_right(scale_sq[0:1] * squares[1 + d], tmp_b)
        out[1 + d] -= (0.5 * scale[1 + d, 0:1]) * mul(left[1 + d], tmp_b[...])

    def sent(d, source, target, send, recv):
        return pltpu.make_async_remote_copy(
            src_ref=source.at[0],
            dst_ref=target.at[1 + (d ^ 1)],
            send_sem=send.at[d],
            recv_sem=recv.at[d ^ 1, 0],
            device_id=device[d],
            device_id_type=MESH,
        )

    def relay_left(first, n):
        part = relay.at[pl.ds(first * rows, n * rows)]
        pltpu.make_async_remote_copy(
            src_ref=part,
            dst_ref=part,
            send_sem=relay_send.at[first],
            recv_sem=relay_recv.at[first],
            device_id=relay_to,
            device_id_type=MESH,
        ).wait_send()

    pl.when(inner)(functools.partial(relay_left, 0, 1))
    pl.when(inner & even)(functools.partial(relay_left, 1, CHUNKS - 1))

    for d in range(6):
        keep_copy(d).wait_send()
        couple_copy(d).wait_send()
        sent(d, *own_copies).wait_send()

    @pl.loop(0, 2 * CHUNKS)
    def _(q):
        earlier = jnp.where(edge, late[0], late[1])
        d, c = jnp.where(lax.rem(q, 2) == 0, earlier, late[2]), q // 2

        @pl.when(awaits(d))
        def _():
            for k in range(PIECES // CHUNKS):
                arrival(
                    d, PIECES // CHUNKS * c + k, squares, s_send, s_recv
                ).wait_recv()

        as_right_chunk(scale_sq[0:1] * squares[1 + d, chunk(c)], tmp_b, 0)
        columns = pl.ds(pl.multiple_of(3 * c * rows, 3 * rows), 3 * rows)
        out[1 + d] -= (0.5 * scale[1 + d, 0:1]) * mul(
            left[1 + d, :, columns], tmp_b[0 : 3 * rows]
        )

    for d in range(6):
        sent(d, *squares_copies).wait_send()


def write_out(result, out_hbm, sem):
    copies = [
        pltpu.make_async_copy(result.at[s], out_hbm.at[s], sem.at[s]) for s in range(7)
    ]
    for copy in copies:
        copy.start()
    for copy in copies:
        copy.wait()


def body(hamiltonian, keep_mask):
    blocks = hamiltonian[0, 0, 0]
    width = blocks.shape[-1]
    sizes = tuple(lax.axis_size(n) for n in ("gx", "gy", "gz"))
    keep = keep_mask[0, 0, 0]
    count = float(sizes[0] * sizes[1] * sizes[2] * width)
    square = (width, width)
    dma = pltpu.SemaphoreType.DMA
    vmem = pltpu.VMEM
    result = pl.pallas_call(
        functools.partial(kernel, sizes, count),
        out_shape=vmem((7, *square), F32),
        in_specs=[
            pl.BlockSpec(memory_space=pltpu.HBM),
            pl.BlockSpec(memory_space=pltpu.SMEM),
        ],
        out_specs=pl.BlockSpec(memory_space=vmem),
        scratch_shapes=[
            vmem((7, *square), F32),
            vmem((6, *square), F32),
            vmem((7, *square), F32),
            vmem((7, *square), F32),
            vmem((7, 8, width), F32),
            vmem((6, 8, width), F32),
            vmem(square, F32),
            vmem((7, width, 3 * width), BF16),
            vmem((6, 3 * width, width), BF16),
            vmem((3 * width, width), BF16),
            vmem((width, 3 * width), BF16),
            vmem((3 * width, width), BF16),
            vmem(square, F32),
            vmem(square, F32),
            vmem((8, width), F32),
            vmem((7, 8, width), F32),
            vmem((sizes[0], 8, 128), F32),
            vmem((sizes[1], 8, 128), F32),
            vmem((sizes[2], 8, 128), F32),
            dma((7,)),
            dma((6,)),
            dma((6,)),
            dma((3,)),
            dma((3,)),
            dma((6,)),
            dma((6,)),
            dma((2,)),
            dma((CHUNKS,)),
            dma((6,)),
            dma((6, PIECES)),
            dma((6,)),
            dma((6, PIECES)),
        ],
        compiler_params=pltpu.CompilerParams(
            collective_id=0, has_side_effects=True, vmem_limit_bytes=56 << 20
        ),
        name="sign_step",
    )(blocks, keep)
    result = pl.pallas_call(
        write_out,
        out_shape=jax.ShapeDtypeStruct((7, *square), F32),
        in_specs=[pl.BlockSpec(memory_space=vmem)],
        out_specs=pl.BlockSpec(memory_space=pltpu.HBM),
        scratch_shapes=[dma((7,))],
        compiler_params=pltpu.CompilerParams(vmem_limit_bytes=6 << 20),
        name="write_out",
    )(result)
    return result[None, None, None]


def solution(mesh):
    placed = (P("gx", "gy", "gz", None, None, None), P("gx", "gy", "gz", None))
    return jax.shard_map(
        body,
        mesh=mesh,
        in_specs=placed,
        out_specs=P("gx", "gy", "gz", None, None, None),
        check_vma=False,
    )
```
